32 devices in a mesh: tok: 4 (over y, x), row: 8 (over z, core).
Axes of the slice: x: 2, y: 2, z: 4, core: 2. Of those that a mesh axis runs over, the one named last changes fastest.
Arguments:
- hidden: bfloat16 [768, 28672], P('tok', 'row'), may hold values from -6 to 6
- resid: bfloat16 [768, 8192], P('tok', 'row'), may hold values from -6 to 6
- down_in: bfloat16 [28672, 256], P('row'), may hold values from -0.03125 to 0.03125
- down_out: bfloat16 [256, 8192], P(None, 'row'), may hold values from -0.375 to 0.375
- up_weight: bfloat16 [8192, 28672], P('row', 'tok'), may hold values from -0.0625 to 0.0625
- start: bfloat16 [28672, 256], P('tok'), may hold values from -6 to 6
Outputs:
- left_basis: float32 [8192, 256], P('row')
- right_basis: float32 [28672, 256], P(('tok', 'row'))
- core: float32 [256, 256], replicated
The draws below stay inside these ranges and needn't reach their ends.
All inputs are finite; a program needn't handle non-finite values.
Results may differ from the reference program's by a relative error of at most 0.0004.
Values sent between devices are 32-bit elements; how exact they have to be, the bound alone decides.
A program may use at most 128 MiB of HBM per device.

```python
import math
import jax
import jax.numpy as jnp
from jax import lax

D = 8192
FF = 28672
FW = 28672
R = 256
RD = 256
ITERS = 2
TOKENS = 768


def rough_field(key, rows, cols):
    values = jax.random.normal(key, (rows, cols), jnp.float32)
    return jnp.clip(values, -6.0, 6.0).astype(jnp.bfloat16)


def draw_hidden(key, part):
    return rough_field(jax.random.fold_in(key, 11), TOKENS, FF)


def draw_resid(key, part):
    return rough_field(jax.random.fold_in(key, 23), TOKENS, D)


def steps_of(key, extent, cuts, low, largest):
    def one(dim, shards_of):
        heights = jax.random.uniform(jax.random.fold_in(jax.random.fold_in(key, 6), dim), (shards_of,), jnp.float32, low / len(cuts), largest / len(cuts))
        return jnp.repeat(jnp.exp(heights), extent[dim] // shards_of).reshape((-1,) + (1,) * (len(extent) - dim - 1))

    gain = one(*cuts[0])
    for cut in cuts[1:]:
        gain = gain * one(*cut)
    return gain


def bell_draw(stream_key, dims, spread, reach, cuts=(), held_as=jnp.bfloat16):
    factor_of = steps_of(stream_key, dims, cuts, -0.22, 0.18) if cuts else 1.0
    entries = jax.random.normal(stream_key, dims, jnp.float32) * spread * factor_of
    return jnp.minimum(jnp.maximum(entries, -reach), reach).astype(held_as)


def setup_inputs(seed: int = 0) -> dict:
    keys = jax.random.split(jax.random.key(seed), 7)
    return {
        "hidden": draw_hidden(jax.random.fold_in(keys[6], 71), 0),
        "resid": draw_resid(jax.random.fold_in(keys[6], 71), 0),
        "down_in": bell_draw(keys[2], (FF, RD), FF ** -0.5, 0.03125, ((0, 8),)),
        "down_out": bell_draw(keys[3], (RD, D), RD ** -0.5, 0.375, ((1, 8),)),
        "up_weight": bell_draw(keys[4], (D, FW), D ** -0.5, 0.0625, ((0, 8), (1, 4))),
        "start": bell_draw(keys[5], (FW, R), 1.0, 6.0, ((0, 4),)),
    }


HIGH = lax.Precision.HIGHEST

def orthonormal(block):
    inner = jnp.dot(block.T, block, precision=HIGH)
    lower = jnp.linalg.cholesky(inner)
    return jax.scipy.linalg.solve_triangular(lower, block.T, lower=True).T

def reference(hidden, resid, down_in, down_out, up_weight, start):
    code = jnp.dot(hidden.astype(jnp.float32), down_in.astype(jnp.float32), preferred_element_type=jnp.float32)
    act_full = resid.astype(jnp.float32) + jnp.dot(code, down_out.astype(jnp.float32), precision=HIGH)

    def whiten(block):
        return jnp.dot(act_full.T, jnp.dot(act_full, block, precision=HIGH), precision=HIGH) / TOKENS
    weight = up_weight.astype(jnp.float32)
    right = start.astype(jnp.float32)
    left = jnp.zeros((D, R), jnp.float32)
    back = jnp.zeros((D, R), jnp.float32)
    for step in range(ITERS):
        image = jnp.dot(weight, right, precision=HIGH)
        left = orthonormal(whiten(image))
        back = whiten(left)
        right = orthonormal(jnp.dot(weight.T, back, precision=HIGH))
    core = jnp.dot(back.T, jnp.dot(weight, right, precision=HIGH), precision=HIGH)
    return (math.sqrt(D) * left, math.sqrt(FW) * right, core)
```

```python
import functools
import math

import jax
import jax.numpy as jnp
from jax import lax
from jax.experimental import pallas as pl
from jax.experimental.pallas import tpu as pltpu
from jax.sharding import PartitionSpec as P

ITERS = 2
HIGH = lax.Precision.HIGHEST
F32 = jnp.float32
BF16 = jnp.bfloat16


def inner(first, second):
    return lax.dot_general(
        first, second, (((0,), (0,)), ((), ())), precision=HIGH, preferred_element_type=F32
    )


def outer(first, second):
    return lax.dot_general(
        first, second, (((1,), (1,)), ((), ())), precision=HIGH, preferred_element_type=F32
    )


def solve_lower(lower, block):
    return jax.scipy.linalg.solve_triangular(lower, block.T, lower=True).T


def activations(hidden, resid, down_in, down_out):
    partial_value = jnp.dot(hidden, down_in, preferred_element_type=F32)
    code = lax.psum(partial_value, "row")
    return resid.astype(F32) + jnp.dot(code, down_out.astype(F32), precision=HIGH)


def feature_space(hidden, resid, down_in, down_out, up_weight, start):
    act_full = activations(hidden, resid, down_in, down_out)
    total_tokens = act_full.shape[0] * lax.axis_size("tok")
    features = up_weight.shape[0] * lax.axis_size("row")
    columns = up_weight.shape[1] * lax.axis_size("tok")

    def whiten(block):
        applied = lax.psum(jnp.dot(act_full, block, precision=HIGH), "row")
        return lax.psum(inner(act_full, applied), "tok") / total_tokens

    weight = up_weight.astype(F32)
    right = start.astype(F32)
    for step in range(ITERS):
        image = lax.psum(jnp.dot(weight, right, precision=HIGH), "tok")
        target = whiten(image)
        lower = jnp.linalg.cholesky(lax.psum(inner(target, target), "row"))
        left = solve_lower(lower, target)
        back = whiten(left)
        share = lax.psum_scatter(inner(weight, back), "row", scatter_dimension=0, tiled=True)
        right_lower = jnp.linalg.cholesky(lax.psum(inner(share, share), ("tok", "row")))
        piece = solve_lower(right_lower, share)
        right = lax.all_gather(piece, "row", axis=0, tiled=True)
    core = lax.psum(inner(back, jnp.dot(weight, right, precision=HIGH)), ("tok", "row"))
    return (math.sqrt(features) * left, math.sqrt(columns) * piece, core)


def dots(first, second, dims):
    def one(x, y):
        return lax.dot_general(x, y, (dims, ((), ())), preferred_element_type=F32)

    return one(first[1], second[0]) + one(first[0], second[1]) + one(first[0], second[0])


NB = 64


def factor_block(table, at):
    size = table.shape[0]
    eye = (
        lax.broadcasted_iota(jnp.int32, (NB, NB), 0) == lax.broadcasted_iota(jnp.int32, (NB, NB), 1)
    ).astype(F32)
    back = (
        lax.broadcasted_iota(jnp.int32, (NB, NB), 0) == lax.broadcasted_iota(jnp.int32, (NB, NB), 1) + 1
    ).astype(F32)
    index = lax.broadcasted_iota(jnp.int32, (8, 2 * NB), 0)
    work = jnp.concatenate([table[at : at + NB, at : at + NB], eye], axis=1)
    groups = [work[k : k + 8, :] for k in range(0, NB, 8)]
    wide = (8, 2 * NB)
    for j in range(0, NB, 2):
        own, spot = divmod(j, 8)
        ones = [jnp.broadcast_to(groups[k][:, j : j + 1], wide) for k in range(own, NB // 8)]
        twos = [jnp.broadcast_to(groups[k][:, j + 1 : j + 2], wide) for k in range(own, NB // 8)]
        row1, row2 = groups[own][spot : spot + 1, :], groups[own][spot + 1 : spot + 2, :]
        a, b = ones[0][spot : spot + 1, :], twos[0][spot : spot + 1, :]
        d = twos[0][spot + 1 : spot + 2, :]
        inverse = 1.0 / (a * d - b * b)
        first = (d * row1 - b * row2) * inverse
        second = (a * row2 - b * row1) * inverse
        for k in range(own, NB // 8):
            change = ones[k - own] * first + twos[k - own] * second
            if k == own:
                change = jnp.where(index > spot + 1, change, 0.0)
            groups[k] = groups[k] - change
    work = jnp.concatenate(groups, axis=0)
    odd = lax.rem(lax.broadcasted_iota(jnp.int32, (NB, 1), 0), 2) == 1
    pivot = jnp.sum(work[:, :NB] * eye, axis=1, keepdims=True)
    cross = jnp.sum(work[:, :NB] * back, axis=1, keepdims=True)
    right = work[:, NB:]
    before = jnp.concatenate([right[:1], right[:-1]], axis=0)
    ratio = jnp.where(odd, cross / jnp.concatenate([pivot[:1], pivot[:-1]], axis=0), 0.0)
    small = (right - ratio * before) * lax.rsqrt(pivot - ratio * cross)
    rows = jnp.dot(small, table[at : at + NB, :], precision=HIGH, preferred_element_type=F32)
    table[at : at + NB, :] = rows
    if at + NB < size:
        below = rows[:, at + NB : size]
        table[at + NB :, :] = table[at + NB :, :] - inner(below, rows)


def set_table(table, gram):
    size = gram.shape[0]
    table[:, :size] = gram
    table[:, size:] = (
        lax.broadcasted_iota(jnp.int32, (size, size), 0)
        == lax.broadcasted_iota(jnp.int32, (size, size), 1)
    ).astype(F32)


def inverse_of(table, gram):
    set_table(table, gram)
    for at in range(0, gram.shape[0], NB):
        factor_block(table, at)
    return table[:, gram.shape[0] :]


MESH = pl.DeviceIdType.MESH
VMEM = pl.BlockSpec(memory_space=pltpu.VMEM)
ANY = pl.BlockSpec(memory_space=pl.ANY)


def place():
    tok, row = lax.axis_index("tok"), lax.axis_index("row")
    return tok, row, row // 2, lax.rem(row, 2)


def other(index, bit):
    if bit == 1:
        return index + 1 - 2 * lax.rem(index, 2)
    return lax.rem(index + 2, 4)


def greet(partners):
    barrier = pltpu.get_barrier_semaphore()
    for partner in partners:
        pl.semaphore_signal(barrier, inc=1, device_id=partner, device_id_type=MESH)
    pl.semaphore_wait(barrier, len(partners))


def remote(src, dst, send_sem, recv_sem, partner):
    return pltpu.make_async_remote_copy(
        src_ref=src, dst_ref=dst, send_sem=send_sem, recv_sem=recv_sem,
        device_id=partner, device_id_type=MESH,
    )


def split_two(block):
    first = block.astype(BF16)
    return first, (block - first.astype(F32)).astype(BF16)


def split_three(block):
    first, rest = block.astype(BF16), None
    rest = block - first.astype(F32)
    second = rest.astype(BF16)
    third = (rest - second.astype(F32)).astype(BF16)
    return first, second, third


def acts_kernel(
    hidden_ref, resid_ref, din_ref, dout_ref, acts_ref, high_ref, low_ref,
    part, inbox, code, base, sum_send, sum_recv, code_send, code_recv, tok_send, tok_recv,
):
    tok, row, _, _ = place()
    rows = hidden_ref.shape[0]
    half = rows // 2
    share = rows // 8
    by_x, by_y = (other(tok, 1), row), (other(tok, 2), row)
    peers = [(tok, lax.rem(row + d, 8)) for d in range(1, 8)]
    greet(peers + [by_x, by_y])

    part[...] = jnp.dot(hidden_ref[...], din_ref[...], preferred_element_type=F32)
    copies = []
    for d, peer in enumerate(peers):
        piece = part.at[pl.ds(pl.multiple_of(peer[1] * share, 8), share)]
        copies.append(remote(piece, inbox.at[d], sum_send.at[d], sum_recv.at[d], peer))
        copies[-1].start()
    mine = pl.ds(pl.multiple_of(row * share, 8), share)
    total = part[mine, :]
    for d in range(7):
        copies[d].wait_recv()
        total += inbox[d]
    code[mine, :] = total
    gathers = []
    for d, peer in enumerate(peers):
        gathers.append(remote(code.at[mine], code.at[mine], code_send.at[d], code_recv.at[d], peer))
        gathers[-1].start()
    for d in range(7):
        source = pl.ds(pl.multiple_of(lax.rem(row + 7 - d, 8) * share, 8), share)
        remote(code.at[source], code.at[source], code_send.at[d], code_recv.at[d], peers[d]).wait_recv()
    first, second, third = split_three(code[...])
    weight = dout_ref[...]
    own = jnp.dot(third, weight, preferred_element_type=F32)
    own += jnp.dot(second, weight, preferred_element_type=F32)
    own += jnp.dot(first, weight, preferred_element_type=F32)
    base[0] = resid_ref[...].astype(F32) + own

    top, bottom = pl.ds(0, half), pl.ds(half, half)

    def send(slot, to, piece, index, partner):
        copy = remote(base.at[slot, piece], base.at[to, piece], tok_send.at[index], tok_recv.at[index], partner)
        copy.start()
        return copy

    moves = [
        send(0, 1, top, 0, by_x),
        send(0, 2, bottom, 1, by_y),
        send(0, 1, bottom, 2, by_x),
        send(0, 2, top, 3, by_y),
    ]

    def emit(slot, group):
        rows_of = pl.ds(pl.multiple_of(group * rows, 16), rows)
        value = base[slot]
        acts_ref[rows_of, :] = value
        high, low = split_two(value)
        high_ref[rows_of, :] = high
        low_ref[rows_of, :] = low

    emit(0, tok)
    moves[0].wait_recv()
    moves.append(send(1, 3, top, 4, by_y))
    moves[1].wait_recv()
    moves.append(send(2, 3, bottom, 5, by_x))
    moves[2].wait_recv()
    emit(1, other(tok, 1))
    moves[3].wait_recv()
    emit(2, other(tok, 2))
    moves[4].wait_recv()
    moves[5].wait_recv()
    emit(3, other(other(tok, 1), 2))
    for copy in copies + gathers + moves:
        copy.wait_send()


def activation_rows(hidden, resid, down_in, down_out):
    rows, width = resid.shape
    rank = down_in.shape[1]
    tokens = 4 * rows
    return pl.pallas_call(
        acts_kernel,
        in_specs=[VMEM] * 4,
        out_specs=[VMEM] * 3,
        out_shape=[
            jax.ShapeDtypeStruct((tokens, width), F32),
            jax.ShapeDtypeStruct((tokens, width), BF16),
            jax.ShapeDtypeStruct((tokens, width), BF16),
        ],
        scratch_shapes=[
            pltpu.VMEM((rows, rank), F32),
            pltpu.VMEM((7, rows // 8, rank), F32),
            pltpu.VMEM((rows, rank), F32),
            pltpu.VMEM((4, rows, width), F32),
            pltpu.SemaphoreType.DMA((7,)),
            pltpu.SemaphoreType.DMA((7,)),
            pltpu.SemaphoreType.DMA((7,)),
            pltpu.SemaphoreType.DMA((7,)),
            pltpu.SemaphoreType.DMA((6,)),
            pltpu.SemaphoreType.DMA((6,)),
        ],
        compiler_params=pltpu.CompilerParams(
            collective_id=1, has_side_effects=True, vmem_limit_bytes=40 * 2**20
        ),
    )(hidden, resid, down_in, down_out)


CUTS = 8
LAG = 2


def applied_kernel(
    high_ref, low_ref, weight_ref, out_ref,
    held, own, inner_in, line_in, stage,
    weight_sem, pair_send, pair_recv, line_send, line_recv, out_sem,
):
    tok, row, z, core = place()
    tokens = high_ref.shape[0]
    _, _, rows, width = own.shape
    steps = own.shape[1]
    cut = rows // CUTS
    sibling = (tok, other(row, 1))
    down, up = (tok, row - 2), (tok, row + 2)
    barrier = pltpu.get_barrier_semaphore()
    pl.semaphore_signal(barrier, inc=1, device_id=sibling, device_id_type=MESH)

    @pl.when(z > 0)
    def _():
        pl.semaphore_signal(barrier, inc=1, device_id=down, device_id_type=MESH)

    @pl.when(z < 3)
    def _():
        pl.semaphore_signal(barrier, inc=1, device_id=up, device_id_type=MESH)

    pl.semaphore_wait(barrier, jnp.where((z == 0) | (z == 3), 2, 3))

    def load(step, which):
        end, mine = which % 2, which // 2
        side = core if mine else 1 - core
        block = 4 * end + 2 * lax.rem(step, 2) + side
        columns = pl.ds(pl.multiple_of(block * width, 128), width)
        return pltpu.make_async_copy(weight_ref.at[:, columns], held.at[which], weight_sem.at[which])

    def pair_copy(step, end):
        slot = lax.rem(step, 2)
        return remote(
            stage.at[slot, end], inner_in.at[end, step], pair_send.at[slot, end],
            pair_recv.at[end, step], sibling,
        )

    def line_copy(end, step, piece, at):
        part = pl.ds(pl.multiple_of(piece * cut, 8), cut)
        return remote(
            own.at[end, step, part], line_in.at[end, step, part], line_send.at[end],
            line_recv.at[end, at], down if end == 0 else up,
        )

    def out_copy(end, step):
        group = step // 2
        part = pl.ds(pl.multiple_of(group * rows, 8), rows)
        return pltpu.make_async_copy(own.at[end, step], out_ref.at[lax.rem(step, 2), part], out_sem.at[step])

    for which in range(4):
        load(0, which).start()

    def multiply(step, which):
        part = pl.ds(pl.multiple_of((step // 2) * rows, 16), rows)
        end = which % 2
        load(step, which).wait()
        weight = held[which]
        value = jnp.dot(low_ref[part, :], weight, preferred_element_type=F32)
        value += jnp.dot(high_ref[part, :], weight, preferred_element_type=F32)
        if which < 2:

            @pl.when(step >= 2)
            def _():
                pair_copy(step - 2, end).wait_send()

            stage[lax.rem(step, 2), end] = value
            pair_copy(step, end).start()
        else:
            own[end, step] = value

        @pl.when(step + 1 < steps)
        def _():
            load(step + 1, which).start()

    def forward(end, at):
        hops = 3 - z if end == 0 else z
        at = at - LAG * hops

        @pl.when((at >= 0) & (at < CUTS * steps))
        def _():
            step, piece = at // CUTS, lax.rem(at, CUTS)
            part = pl.ds(pl.multiple_of(piece * cut, 8), cut)

            @pl.when(piece == 0)
            def _():
                pair_copy(step, end).wait_recv()

            own[end, step, part, :] = own[end, step, part, :] + inner_in[end, step, part, :]

            @pl.when(hops > 0)
            def _():
                line_copy(end, step, piece, at).wait_recv()
                own[end, step, part, :] = own[end, step, part, :] + line_in[end, step, part, :]

            @pl.when(hops < 3)
            def _():
                line_copy(end, step, piece, at).start()

            @pl.when((hops == 3) & (piece == CUTS - 1))
            def _():
                out_copy(end, step).start()

    for which in range(4):
        multiply(0, which)

    def one(step, carry):
        for piece in range(CUTS):
            if piece % 2 == 0:

                @pl.when(step + 1 < steps)
                def _():
                    multiply(step + 1, piece // 2)

            for end in range(2):
                forward(end, step * CUTS + piece)
        return carry

    lax.fori_loop(0, steps + -(-3 * LAG // CUTS), one, 0)

    for end in range(2):
        hops = 3 - z if end == 0 else z
        for step in (steps - 2, steps - 1):
            pair_copy(step, end).wait_send()

        @pl.when(hops < 3)
        def _():
            remote(
                own.at[end], line_in.at[end], line_send.at[end], line_recv.at[end, 0],
                down if end == 0 else up,
            ).wait_send()

        @pl.when(hops == 3)
        def _():
            for step in range(steps):
                out_copy(end, step).wait()


def applied_sums(high, low, weight):
    tokens, depth = high.shape
    rows = tokens // 4
    width = weight.shape[1] // 8
    steps = 8
    return pl.pallas_call(
        applied_kernel,
        in_specs=[VMEM, VMEM, ANY],
        out_specs=ANY,
        out_shape=jax.ShapeDtypeStruct((2, tokens, width), F32),
        scratch_shapes=[
            pltpu.VMEM((4, depth, width), BF16),
            pltpu.VMEM((2, steps, rows, width), F32),
            pltpu.VMEM((2, steps, rows, width), F32),
            pltpu.VMEM((2, steps, rows, width), F32),
            pltpu.VMEM((2, 2, rows, width), F32),
            pltpu.SemaphoreType.DMA((4,)),
            pltpu.SemaphoreType.DMA((2, 2)),
            pltpu.SemaphoreType.DMA((2, steps)),
            pltpu.SemaphoreType.DMA((2,)),
            pltpu.SemaphoreType.DMA((2, steps * CUTS)),
            pltpu.SemaphoreType.DMA((steps,)),
        ],
        compiler_params=pltpu.CompilerParams(
            collective_id=2, has_side_effects=True, vmem_limit_bytes=56 * 2**20
        ),
        cost_estimate=pl.CostEstimate(
            flops=4 * tokens * depth * weight.shape[1],
            bytes_accessed=500 * 2**20,
            transcendentals=0,
        ),
    )(high, low, weight)


TRI = ((0, 0), (1, 0), (1, 1), (2, 0), (2, 1), (2, 2))


def basis_kernel(
    blocks_ref, gram_ref, imaged_ref, high_ref, low_ref, left_ref, right_ref, core_ref,
    parts, square, pair_in, sum_in, whole, halves, tall, sent, landed, table,
    pair_send, pair_recv, sum_send, sum_recv, line_send, line_recv, tok_send, tok_recv, end_send, end_recv,
    *, features, columns,
):
    tok, row, z, core = place()
    tokens, rank = imaged_ref.shape
    width = blocks_ref.shape[2]
    third = tokens // 3
    piece = 6 * third // 16
    half = 8 * piece
    end = z // 2
    holds = (z == 0) | (z == 3)
    sibling = (tok, other(row, 1))
    toks = [tok, other(tok, 1), other(tok, 2), other(other(tok, 1), 2)]
    barrier = pltpu.get_barrier_semaphore()
    near = [sibling] + [(t, row) for t in toks[1:]] + [(tok, lax.rem(row + d, 8)) for d in (2, 4, 6)]
    for partner in near:
        pl.semaphore_signal(barrier, inc=1, device_id=partner, device_id_type=MESH)
    far = [(t, 6 - 2 * z + core) for t in toks[1:]]

    @pl.when(holds)
    def _():
        for partner in far:
            pl.semaphore_signal(barrier, inc=1, device_id=partner, device_id_type=MESH)

    pl.semaphore_wait(barrier, jnp.where(holds, 10, 7))

    mine = pl.ds(pl.multiple_of(core * half, 8), half)
    theirs = pl.ds(pl.multiple_of((1 - core) * half, 8), half)
    pair = remote(square.at[theirs], pair_in, pair_send.at[0], pair_recv.at[0], sibling)

    @pl.when(holds)
    def _():
        for at in range(2):
            first, second = split_two(blocks_ref[at])
            parts[0, at] = first
            parts[1, at] = second
        for n, (i, j) in enumerate(TRI):
            a, b = pl.ds(i * third, third), pl.ds(j * third, third)
            square[pl.ds(n * third, third), :] = sum(
                dots((parts[0, at, a], parts[1, at, a]), (parts[0, at, b], parts[1, at, b]), ((1,), (1,)))
                for at in range(2)
            )
        pair.start()

    gram_parts = split_two(gram_ref[...])
    block = imaged_ref[...] / tokens
    tall[0] = dots(gram_parts, split_two(block), ((1,), (0,)))
    set_table(table, inner(block, tall[0]))

    def spot(to_core, to_tok, to_end):
        return pl.ds(pl.multiple_of(to_core * half + (to_tok * 2 + to_end) * piece, 8), piece)

    def sum_copy(d):
        to_tok = toks[d // 2]
        to_end = 1 - end if d % 2 else end
        return remote(
            square.at[spot(core, to_tok, to_end)], sum_in.at[d], sum_send.at[d], sum_recv.at[d],
            (to_tok, 6 * to_end + core),
        )

    @pl.when(holds)
    def _():
        pair.wait_recv()
        square[mine, :] = square[mine, :] + pair_in[...]
        for d in (7, 5, 3, 1, 6, 4, 2):
            sum_copy(d).start()

    factor_block(table, 0)
    factor_block(table, NB)

    here = spot(core, tok, end)

    def line_copy(i):
        to = (3 - i) + end * (2 * i - 3)
        return remote(whole.at[here], whole.at[here], line_send.at[i], line_recv.at[end], (tok, 2 * to + core))

    def tok_copy(source_end, d):
        place_of = spot(core, tok, source_end)
        return remote(
            whole.at[place_of], whole.at[place_of], tok_send.at[source_end, d], tok_recv.at[source_end, d],
            (toks[d], row),
        )

    @pl.when(holds)
    def _():
        total = square[here, :]
        for d in range(1, 8):
            sum_copy(d).wait_recv()
            total += sum_in[d]
        whole[here, :] = total
        for i in range(3):
            line_copy(i).start()
        for d in (3, 1, 2):
            tok_copy(end, d).start()

    factor_block(table, 2 * NB)
    for source in range(2):

        @pl.when(z != 3 * source)
        def _():
            landing = spot(core, tok, source)
            remote(
                whole.at[landing], whole.at[landing], line_send.at[0], line_recv.at[source], sibling
            ).wait_recv()
            for d in (3, 1, 2):
                tok_copy(source, d).start()

    factor_block(table, 3 * NB)
    tall[1] = outer(tall[0], table[:, rank:]) / tokens
    for source in range(2):
        for d in (1, 2, 3):
            landing = spot(core, toks[d], source)
            remote(
                whole.at[landing], whole.at[landing], tok_send.at[source, d], tok_recv.at[source, d], sibling
            ).wait_recv()
    last = remote(whole.at[mine], whole.at[mine], pair_send.at[1], pair_recv.at[1], sibling)
    last.start()
    remote(whole.at[theirs], whole.at[theirs], pair_send.at[1], pair_recv.at[1], sibling).wait_recv()
    first, second = split_two(whole[...])
    halves[0] = first
    halves[1] = second

    def squared(to, block):
        pieces = [split_two(block[i * third : (i + 1) * third, :]) for i in range(3)]
        for i in range(3):
            total = None
            for j in range(3):
                n = TRI.index((max(i, j), min(i, j)))
                at = pl.ds(n * third, third)
                dims = ((1,), (0,)) if i >= j else ((0,), (0,))
                term = dots((halves[0, at], halves[1, at]), pieces[j], dims)
                total = term if total is None else total + term
            tall[to, pl.ds(i * third, third), :] = total

    block = tall[1]
    squared(0, block)
    inverse = inverse_of(table, inner(block, tall[0]))
    tall[1] = outer(tall[0], inverse) / tokens

    block = tall[1]
    tall[0] = dots(gram_parts, split_two(block), ((1,), (0,)))
    inverse = inverse_of(table, inner(block, tall[0]))
    coef = split_two(outer(block, inverse))
    tall[1] = outer(tall[0], inverse) / tokens

    block = tall[1]
    ends = split_two(block)
    carry = remote(
        sent, landed, end_send.at[0], end_recv.at[0],
        (tok, jnp.where(z < 2, 2, 4) + core),
    )

    @pl.when(holds)
    def _():
        away = 1 - end
        sent[...] = dots((parts[0, away], parts[1, away]), ends, ((0,), (0,)))
        carry.start()
        landed[...] = dots((parts[0, end], parts[1, end]), ends, ((0,), (0,)))

    left_ref[...] = math.sqrt(features) * dots((high_ref[...], low_ref[...]), coef, ((0,), (0,)))
    squared(0, block)
    gram = inner(block, tall[0])
    inverse = inverse_of(table, gram)
    core_ref[...] = outer(gram, inverse)

    @pl.when(z == 1)
    def _():
        carry.wait_recv()

    @pl.when(z == 2)
    def _():
        carry.wait_recv()

    right_ref[...] = math.sqrt(columns) * outer(landed[...], inverse)

    @pl.when(holds)
    def _():
        carry.wait_send()
        pair.wait_send()
        for d in range(1, 8):
            sum_copy(d).wait_send()
        for i in range(3):
            line_copy(i).wait_send()

    for source in range(2):
        for d in (1, 2, 3):
            tok_copy(source, d).wait_send()
    last.wait_send()


def bases(blocks, gram, imaged, high, low, features, columns):
    tokens, rank = imaged.shape
    width, depth = blocks.shape[2], high.shape[1]
    third = tokens // 3
    dma = pltpu.SemaphoreType.DMA
    return pl.pallas_call(
        functools.partial(basis_kernel, features=features, columns=columns),
        in_specs=[VMEM] * 5,
        out_specs=[VMEM] * 3,
        out_shape=[
            jax.ShapeDtypeStruct((depth, rank), F32),
            jax.ShapeDtypeStruct((width, rank), F32),
            jax.ShapeDtypeStruct((rank, rank), F32),
        ],
        scratch_shapes=[
            pltpu.VMEM((2, 2, tokens, width), BF16),
            pltpu.VMEM((6 * third, third), F32),
            pltpu.VMEM((3 * third, third), F32),
            pltpu.VMEM((8, 6 * third // 16, third), F32),
            pltpu.VMEM((6 * third, third), F32),
            pltpu.VMEM((2, 6 * third, third), BF16),
            pltpu.VMEM((2, tokens, rank), F32),
            pltpu.VMEM((width, rank), F32),
            pltpu.VMEM((width, rank), F32),
            pltpu.VMEM((rank, 2 * rank), F32),
            dma((2,)), dma((2,)), dma((8,)), dma((8,)), dma((3,)), dma((2,)),
            dma((2, 4)), dma((2, 4)), dma((1,)), dma((1,)),
        ],
        compiler_params=pltpu.CompilerParams(
            collective_id=3, has_side_effects=True, vmem_limit_bytes=56 * 2**20
        ),
    )(blocks, gram, imaged, high, low)


def token_space(hidden, resid, down_in, down_out, up_weight, start):
    tokens = hidden.shape[0] * 4
    features = up_weight.shape[0] * 8
    columns = up_weight.shape[1] * 4

    image = jnp.dot(up_weight, start, preferred_element_type=F32)
    acts, high, low = activation_rows(hidden, resid, down_in, down_out)
    gram = dots((high, low), (high, low), ((1,), (1,))) / 4
    sums = jnp.concatenate([gram, jnp.dot(acts, image, precision=HIGH)], axis=1)
    sums = lax.psum(sums, ("tok", "row"))
    blocks = applied_sums(high, low, up_weight)
    return bases(blocks, sums[:, :tokens], sums[:, tokens:], high, low, features, columns)


def shards(hidden, *rest):
    tokens = hidden.shape[0] * lax.axis_size("tok")
    if tokens > 1024 or (lax.axis_size("tok"), lax.axis_size("row")) != (4, 8):
        return feature_space(hidden, *rest)
    return token_space(hidden, *rest)


def solution(mesh):
    placed = (
        P("tok", "row"),
        P("tok", "row"),
        P("row", None),
        P(None, "row"),
        P("row", "tok"),
        P("tok", None),
    )
    return jax.shard_map(
        shards,
        mesh=mesh,
        in_specs=placed,
        out_specs=(P("row", None), P(("tok", "row"), None), P()),
        check_vma=False,
    )
```

```python
import functools
import math

import jax
import jax.numpy as jnp
from jax import lax
from jax.experimental import pallas as pl
from jax.experimental.pallas import tpu as pltpu
from jax.sharding import PartitionSpec as P

ITERS = 2
HIGH = lax.Precision.HIGHEST
F32 = jnp.float32
BF16 = jnp.bfloat16


def inner(first, second):
    return lax.dot_general(
        first, second, (((0,), (0,)), ((), ())), precision=HIGH, preferred_element_type=F32
    )


def outer(first, second):
    return lax.dot_general(
        first, second, (((1,), (1,)), ((), ())), precision=HIGH, preferred_element_type=F32
    )


def solve_lower(lower, block):
    return jax.scipy.linalg.solve_triangular(lower, block.T, lower=True).T


def activations(hidden, resid, down_in, down_out):
    partial_value = jnp.dot(hidden, down_in, preferred_element_type=F32)
    code = lax.psum(partial_value, "row")
    return resid.astype(F32) + jnp.dot(code, down_out.astype(F32), precision=HIGH)


def feature_space(hidden, resid, down_in, down_out, up_weight, start):
    act_full = activations(hidden, resid, down_in, down_out)
    total_tokens = act_full.shape[0] * lax.axis_size("tok")
    features = up_weight.shape[0] * lax.axis_size("row")
    columns = up_weight.shape[1] * lax.axis_size("tok")

    def whiten(block):
        applied = lax.psum(jnp.dot(act_full, block, precision=HIGH), "row")
        return lax.psum(inner(act_full, applied), "tok") / total_tokens

    weight = up_weight.astype(F32)
    right = start.astype(F32)
    for step in range(ITERS):
        image = lax.psum(jnp.dot(weight, right, precision=HIGH), "tok")
        target = whiten(image)
        lower = jnp.linalg.cholesky(lax.psum(inner(target, target), "row"))
        left = solve_lower(lower, target)
        back = whiten(left)
        share = lax.psum_scatter(inner(weight, back), "row", scatter_dimension=0, tiled=True)
        right_lower = jnp.linalg.cholesky(lax.psum(inner(share, share), ("tok", "row")))
        piece = solve_lower(right_lower, share)
        right = lax.all_gather(piece, "row", axis=0, tiled=True)
    core = lax.psum(inner(back, jnp.dot(weight, right, precision=HIGH)), ("tok", "row"))
    return (math.sqrt(features) * left, math.sqrt(columns) * piece, core)


def dots(first, second, dims):
    def one(x, y):
        return lax.dot_general(x, y, (dims, ((), ())), preferred_element_type=F32)

    return one(first[1], second[0]) + one(first[0], second[1]) + one(first[0], second[0])


NB = 64


def factor_block(table, at):
    size = table.shape[0]
    eye = (
        lax.broadcasted_iota(jnp.int32, (NB, NB), 0) == lax.broadcasted_iota(jnp.int32, (NB, NB), 1)
    ).astype(F32)
    back = (
        lax.broadcasted_iota(jnp.int32, (NB, NB), 0) == lax.broadcasted_iota(jnp.int32, (NB, NB), 1) + 1
    ).astype(F32)
    index = lax.broadcasted_iota(jnp.int32, (8, 2 * NB), 0)
    work = jnp.concatenate([table[at : at + NB, at : at + NB], eye], axis=1)
    groups = [work[k : k + 8, :] for k in range(0, NB, 8)]
    wide = (8, 2 * NB)
    for j in range(0, NB, 2):
        own, spot = divmod(j, 8)
        ones = [jnp.broadcast_to(groups[k][:, j : j + 1], wide) for k in range(own, NB // 8)]
        twos = [jnp.broadcast_to(groups[k][:, j + 1 : j + 2], wide) for k in range(own, NB // 8)]
        row1, row2 = groups[own][spot : spot + 1, :], groups[own][spot + 1 : spot + 2, :]
        a, b = ones[0][spot : spot + 1, :], twos[0][spot : spot + 1, :]
        d = twos[0][spot + 1 : spot + 2, :]
        inverse = 1.0 / (a * d - b * b)
        first = (d * row1 - b * row2) * inverse
        second = (a * row2 - b * row1) * inverse
        for k in range(own, NB // 8):
            change = ones[k - own] * first + twos[k - own] * second
            if k == own:
                change = jnp.where(index > spot + 1, change, 0.0)
            groups[k] = groups[k] - change
    work = jnp.concatenate(groups, axis=0)
    odd = lax.rem(lax.broadcasted_iota(jnp.int32, (NB, 1), 0), 2) == 1
    pivot = jnp.sum(work[:, :NB] * eye, axis=1, keepdims=True)
    cross = jnp.sum(work[:, :NB] * back, axis=1, keepdims=True)
    right = work[:, NB:]
    before = jnp.concatenate([right[:1], right[:-1]], axis=0)
    ratio = jnp.where(odd, cross / jnp.concatenate([pivot[:1], pivot[:-1]], axis=0), 0.0)
    small = (right - ratio * before) * lax.rsqrt(pivot - ratio * cross)
    rows = jnp.dot(small, table[at : at + NB, :], precision=HIGH, preferred_element_type=F32)
    table[at : at + NB, :] = rows
    if at + NB < size:
        below = rows[:, at + NB : size]
        table[at + NB :, :] = table[at + NB :, :] - inner(below, rows)


def set_table(table, gram):
    size = gram.shape[0]
    table[:, :size] = gram
    table[:, size:] = (
        lax.broadcasted_iota(jnp.int32, (size, size), 0)
        == lax.broadcasted_iota(jnp.int32, (size, size), 1)
    ).astype(F32)


def inverse_of(table, gram):
    set_table(table, gram)
    for at in range(0, gram.shape[0], NB):
        factor_block(table, at)
    return table[:, gram.shape[0] :]


MESH = pl.DeviceIdType.MESH
VMEM = pl.BlockSpec(memory_space=pltpu.VMEM)
ANY = pl.BlockSpec(memory_space=pl.ANY)


def place():
    tok, row = lax.axis_index("tok"), lax.axis_index("row")
    return tok, row, row // 2, lax.rem(row, 2)


def other(index, bit):
    if bit == 1:
        return index + 1 - 2 * lax.rem(index, 2)
    return lax.rem(index + 2, 4)


def greet(partners):
    barrier = pltpu.get_barrier_semaphore()
    for partner in partners:
        pl.semaphore_signal(barrier, inc=1, device_id=partner, device_id_type=MESH)
    pl.semaphore_wait(barrier, len(partners))


def remote(src, dst, send_sem, recv_sem, partner):
    return pltpu.make_async_remote_copy(
        src_ref=src, dst_ref=dst, send_sem=send_sem, recv_sem=recv_sem,
        device_id=partner, device_id_type=MESH,
    )


def split_two(block):
    first = block.astype(BF16)
    return first, (block - first.astype(F32)).astype(BF16)


def split_three(block):
    first, rest = block.astype(BF16), None
    rest = block - first.astype(F32)
    second = rest.astype(BF16)
    third = (rest - second.astype(F32)).astype(BF16)
    return first, second, third


def acts_kernel(
    hidden_ref, resid_ref, din_ref, dout_ref, acts_ref,
    part, inbox, code, sum_send, sum_recv, code_send, code_recv,
):
    tok, row, _, _ = place()
    share = hidden_ref.shape[0] // 8
    peers = [(tok, lax.rem(row + d, 8)) for d in range(1, 8)]
    greet(peers)

    part[...] = jnp.dot(hidden_ref[...], din_ref[...], preferred_element_type=F32)
    copies = []
    for d, peer in enumerate(peers):
        piece = part.at[pl.ds(pl.multiple_of(peer[1] * share, 8), share)]
        copies.append(remote(piece, inbox.at[d], sum_send.at[d], sum_recv.at[d], peer))
        copies[-1].start()
    mine = pl.ds(pl.multiple_of(row * share, 8), share)
    total = part[mine, :]
    for d in range(7):
        copies[d].wait_recv()
        total += inbox[d]
    code[mine, :] = total
    gathers = []
    for d, peer in enumerate(peers):
        gathers.append(remote(code.at[mine], code.at[mine], code_send.at[d], code_recv.at[d], peer))
        gathers[-1].start()
    for d in range(7):
        source = pl.ds(pl.multiple_of(lax.rem(row + 7 - d, 8) * share, 8), share)
        remote(code.at[source], code.at[source], code_send.at[d], code_recv.at[d], peers[d]).wait_recv()
    first, second, third = split_three(code[...])
    weight = dout_ref[...]
    own = jnp.dot(third, weight, preferred_element_type=F32)
    own += jnp.dot(second, weight, preferred_element_type=F32)
    own += jnp.dot(first, weight, preferred_element_type=F32)
    acts_ref[...] = resid_ref[...].astype(F32) + own
    for copy in copies + gathers:
        copy.wait_send()


def activation_rows(hidden, resid, down_in, down_out):
    rows, width = resid.shape
    rank = down_in.shape[1]
    dma = pltpu.SemaphoreType.DMA
    return pl.pallas_call(
        acts_kernel,
        in_specs=[VMEM] * 4,
        out_specs=VMEM,
        out_shape=jax.ShapeDtypeStruct((rows, width), F32),
        scratch_shapes=[
            pltpu.VMEM((rows, rank), F32),
            pltpu.VMEM((7, rows // 8, rank), F32),
            pltpu.VMEM((rows, rank), F32),
            dma((7,)), dma((7,)), dma((7,)), dma((7,)),
        ],
        compiler_params=pltpu.CompilerParams(
            collective_id=1, has_side_effects=True, vmem_limit_bytes=24 * 2**20
        ),
    )(hidden, resid, down_in, down_out)


CUTS = 8
LAG = 2


FIRST = 28
HOP = 6
SPREAD = 49
STEP = 4


def applied_kernel(
    own_ref, weight_ref, start_ref, out_ref, high_ref, low_ref, packed_ref,
    base, held, begin, image, own, inner_in, line_in, stage,
    gp, xp, own_x, inner_x, line_x, stage_x, x_in,
    move_send, move_recv, weight_sem, begin_sem, pair_send, pair_recv, line_send, line_recv, out_sem,
    xp_send, xp_recv, xl_send, xl_recv, xs_send, xs_recv, bc_send, bc_recv, tk_send, tk_recv, last_send, last_recv,
):
    tok, row, z, core = place()
    rows = own_ref.shape[0]
    _, steps, _, width = own.shape
    tokens = 4 * rows
    rank = begin.shape[2]
    cut = rows // CUTS
    quarter, strip = rows // 4, rows // 4 * rank // tokens
    sibling = (tok, other(row, 1))
    toks = [tok, other(tok, 1), other(tok, 2), other(other(tok, 1), 2)]
    by_x, by_y = (toks[1], row), (toks[2], row)
    down, up = (tok, row - 2), (tok, row + 2)
    barrier = pltpu.get_barrier_semaphore()
    for partner in [sibling] + [(t, row) for t in toks[1:]]:
        pl.semaphore_signal(barrier, inc=1, device_id=partner, device_id_type=MESH)

    @pl.when(z > 0)
    def _():
        pl.semaphore_signal(barrier, inc=1, device_id=down, device_id_type=MESH)

    @pl.when(z < 3)
    def _():
        pl.semaphore_signal(barrier, inc=1, device_id=up, device_id_type=MESH)

    pl.semaphore_wait(barrier, jnp.where((z == 0) | (z == 3), 5, 6))

    def block_of(step, which):
        side = core if which // 2 else 1 - core
        return 4 * (which % 2) + 2 * lax.rem(step, 2) + side

    def load(step, which):
        columns = pl.ds(pl.multiple_of(block_of(step, which) * width, 128), width)
        return pltpu.make_async_copy(weight_ref.at[:, columns], held.at[which % 2], weight_sem.at[which % 2])

    def load_begin(step, which):
        lines = pl.ds(pl.multiple_of(block_of(step, which) * width, 16), width)
        return pltpu.make_async_copy(start_ref.at[lines], begin.at[which % 2], begin_sem.at[which % 2])

    for which in range(2):
        load(0, which).start()
        load_begin(0, which).start()

    half = rows // 2
    top, bottom = pl.ds(0, half), pl.ds(half, half)

    def move(index):
        source, to, piece, partner = (
            (own_ref, 0, top, by_x),
            (own_ref, 1, bottom, by_y),
            (own_ref, 0, bottom, by_x),
            (own_ref, 1, top, by_y),
            (base.at[0], 2, top, by_y),
            (base.at[1], 2, bottom, by_x),
        )[index]
        return remote(
            source.at[piece], base.at[to, piece], move_send.at[index], move_recv.at[index], partner
        )

    for index in range(4):
        move(index).start()

    def emit(value, group):
        at = pl.ds(pl.multiple_of(group * rows, 16), rows)
        first, second = split_two(value)
        high_ref[at, :] = first
        low_ref[at, :] = second

    emit(own_ref[...], tok)
    image[...] = jnp.zeros_like(image)

    def group_of(step):
        slot = step // 2
        across = lax.rem(lax.rem(tok, 2) + lax.rem(slot, 2), 2)
        return 2 * lax.rem(tok // 2 + slot // 2, 2) + across

    def pair_copy(step, end):
        return remote(
            stage.at[end], inner_in.at[end, step], pair_send.at[end], pair_recv.at[end, step], sibling
        )

    def line_copy(end, step, piece, at):
        part = pl.ds(pl.multiple_of(piece * cut, 8), cut)
        return remote(
            own.at[end, step, part], line_in.at[end, step, part], line_send.at[end],
            line_recv.at[end, at], down if end == 0 else up,
        )

    def out_copy(end, step):
        part = pl.ds(pl.multiple_of(group_of(step) * rows, 8), rows)
        return pltpu.make_async_copy(own.at[end, step], out_ref.at[lax.rem(step, 2), part], out_sem.at[step])

    def multiply(step, which):
        part = pl.ds(pl.multiple_of(group_of(step) * rows, 16), rows)
        end = which % 2
        load(step, which).wait()
        weight = held[which % 2]
        value = jnp.dot(low_ref[part, :], weight, preferred_element_type=F32)
        value += jnp.dot(high_ref[part, :], weight, preferred_element_type=F32)
        if which < 2:

            @pl.when(step >= 1)
            def _():
                pair_copy(step - 1, end).wait_send()

            stage[end] = value
            pair_copy(step, end).start()
        else:
            own[end, step] = value

        @pl.when(step < 2)
        def _():
            load_begin(step, which).wait()
            image[...] = image[...] + jnp.dot(
                held[which % 2], begin[which % 2], preferred_element_type=F32
            )

        following, next_which = (step, which + 2) if which < 2 else (step + 1, which - 2)

        @pl.when(following < steps)
        def _():
            load(following, next_which).start()

        @pl.when(following < 2)
        def _():
            load_begin(following, next_which).start()

    hops_of = [3 - z, z]

    def forward(end, at):
        hops = hops_of[end]
        at = at - LAG * hops

        @pl.when((at >= 0) & (at < CUTS * steps))
        def _():
            step, piece = at // CUTS, lax.rem(at, CUTS)
            part = pl.ds(pl.multiple_of(piece * cut, 8), cut)

            @pl.when(piece == 0)
            def _():
                pair_copy(step, end).wait_recv()

            own[end, step, part, :] = own[end, step, part, :] + inner_in[end, step, part, :]

            @pl.when(hops > 0)
            def _():
                line_copy(end, step, piece, at).wait_recv()
                own[end, step, part, :] = own[end, step, part, :] + line_in[end, step, part, :]

            @pl.when(hops < 3)
            def _():
                line_copy(end, step, piece, at).start()

            @pl.when((hops == 3) & (piece == CUTS - 1))
            def _():
                out_copy(end, step).start()

    def x_pair(end):
        return remote(stage_x.at[end], inner_x.at[end], xp_send.at[end], xp_recv.at[end], sibling)

    def x_line(end):
        return remote(
            own_x.at[end], line_x.at[end], xl_send.at[end], xl_recv.at[end], down if end == 0 else up
        )

    def x_sum(end, d):
        piece = pl.ds(pl.multiple_of(quarter + strip * toks[d], 8), strip)
        return remote(own_x.at[end, piece], x_in.at[d - 1], xs_send.at[d - 1], xs_recv.at[d - 1], (toks[d], row))

    def spread(end):
        piece = packed_ref.at[end, core, tok]
        return remote(piece, piece, bc_send.at[end], bc_recv.at[end], up if end == 0 else down)

    def token_spread(end, d):
        piece = packed_ref.at[end, core, tok]
        return remote(piece, piece, tk_send.at[end, d], tk_recv.at[end, d], (toks[d], row))

    def token_landing(end, d):
        piece = packed_ref.at[end, core, toks[d]]
        return remote(piece, piece, tk_send.at[end, d], tk_recv.at[end, d], (toks[d], row))

    def last_copy(end, side):
        piece = packed_ref.at[end, side]
        return remote(piece, piece, last_send.at[end], last_recv.at[end], sibling)

    def x_fill():
        for end in range(2):
            for target, side in ((own_x, core), (stage_x, 1 - core)):
                place_of = 2 * end + side
                at = pl.ds(pl.multiple_of(place_of * quarter, 8), quarter)
                target[end, :quarter, :] = gp[at, :]
                for c in range(4):
                    for m in range(tokens // rank):
                        lines = pl.ds(pl.multiple_of(place_of * rows + c * quarter + m * strip, 8), strip)
                        target[end, quarter + c * strip : quarter + (c + 1) * strip, m * rank : (m + 1) * rank] = xp[
                            lines, :
                        ]
            x_pair(end).start()

    def small(step, piece):
        def on(when, extra, action):
            if piece == when % CUTS:
                pl.when((step == when // CUTS) & extra)(action)

        def arrive_first():
            for index in (0, 1):
                move(index).wait_recv()
                move(4 + index).start()

        def arrive_x():
            move(2).wait_recv()
            emit(base[0], toks[1])

        def arrive_y():
            move(3).wait_recv()
            emit(base[1], toks[2])

        def arrive_diagonal():
            move(4).wait_recv()
            move(5).wait_recv()
            emit(base[2], toks[3])

        def gram():
            mine = pl.ds(pl.multiple_of(tok * rows, 16), rows)
            gp[...] = dots((high_ref[mine, :], low_ref[mine, :]), (high_ref[...], low_ref[...]), ((1,), (1,)))

        def imaged():
            xp[...] = dots((high_ref[...], low_ref[...]), split_two(image[...]), ((1,), (0,)))

        always = step >= 0
        on(4, always, arrive_first)
        on(7, always, arrive_x)
        on(12, always, arrive_y)
        on(20, always, arrive_diagonal)
        on(24, always, gram)
        on(25, always, imaged)
        on(26, always, x_fill)
        for end in range(2):
            hops = hops_of[end]

            def joined(end=end):
                x_pair(end).wait_recv()
                own_x[end] = own_x[end] + inner_x[end]

            on(FIRST, always, joined)

            def passed(end=end):
                x_line(end).wait_recv()
                own_x[end] = own_x[end] + line_x[end]

            def split_start(end=end):
                passed(end)
                for d in (3, 1, 2):
                    x_sum(end, d).start()

            def passed_on(end=end):
                passed(end)
                x_line(end).start()

            on(FIRST, hops == 0, lambda end=end: x_line(end).start())
            on(FIRST + HOP, hops == 1, passed_on)
            on(FIRST + 2 * HOP, hops == 2, passed_on)
            on(FIRST + 3 * HOP, hops == 3, split_start)

            def to_tokens(end=end):
                for d in (3, 1, 2):
                    token_spread(end, d).start()

            def packed(end=end):
                at = pl.ds(pl.multiple_of(quarter + strip * tok, 8), strip)
                total = own_x[end, at, :]
                for d in (1, 2, 3):
                    x_sum(end, d).wait_recv()
                    total += x_in[d - 1]
                packed_ref[end, core, tok, :quarter, :] = own_x[end, :quarter, :]
                packed_ref[end, core, tok, quarter:, :] = total
                spread(end).start()
                to_tokens(end)

            def relay(end=end):
                spread(end).wait_recv()
                spread(end).start()
                to_tokens(end)

            def relay_end(end=end):
                spread(end).wait_recv()
                to_tokens(end)

            on(SPREAD, hops == 3, packed)
            on(SPREAD + STEP, hops == 2, relay)
            on(SPREAD + 2 * STEP, hops == 1, relay)
            on(SPREAD + 3 * STEP, hops == 0, relay_end)

        def share_out():
            for end in range(2):
                for d in (1, 2, 3):
                    token_landing(end, d).wait_recv()
                last_copy(end, core).start()

        on(8 * CUTS + 3, always, share_out)

    for which in range(4):
        multiply(0, which)

    def one(step, carry):
        for piece in range(CUTS):
            for which in range(4):
                if piece == which * CUTS // 4:

                    @pl.when(step + 1 < steps)
                    def _():
                        multiply(step + 1, which)

            for end in range(2):
                forward(end, step * CUTS + piece)
            small(step, piece)
        return carry

    lax.fori_loop(0, steps + 1, one, 0)

    for index in range(6):
        move(index).wait_send()
    for end in range(2):
        hops = hops_of[end]
        last_copy(end, 1 - core).wait_recv()
        last_copy(end, core).wait_send()
        x_pair(end).wait_send()
        for d in (1, 2, 3):
            token_spread(end, d).wait_send()
        pair_copy(steps - 1, end).wait_send()

        @pl.when(hops < 3)
        def _():
            x_line(end).wait_send()
            remote(
                own.at[end], line_in.at[end], line_send.at[end], line_recv.at[end, 0],
                down if end == 0 else up,
            ).wait_send()

        @pl.when(hops > 0)
        def _():
            spread(end).wait_send()

        @pl.when(hops == 3)
        def _():
            for d in (1, 2, 3):
                x_sum(end, d).wait_send()
            for step in range(steps):
                out_copy(end, step).wait()


def applied_sums(acts, weight, start):
    rows, depth = acts.shape
    tokens = 4 * rows
    width = weight.shape[1] // 8
    rank = start.shape[1]
    steps = 8
    quarter = rows // 4
    strip = quarter * rank // tokens
    slab = quarter + 4 * strip
    dma = pltpu.SemaphoreType.DMA
    return pl.pallas_call(
        applied_kernel,
        in_specs=[VMEM, ANY, ANY],
        out_specs=[ANY, VMEM, VMEM, VMEM],
        out_shape=[
            jax.ShapeDtypeStruct((2, tokens, width), F32),
            jax.ShapeDtypeStruct((tokens, depth), BF16),
            jax.ShapeDtypeStruct((tokens, depth), BF16),
            jax.ShapeDtypeStruct((2, 2, 4, quarter + strip, tokens), F32),
        ],
        scratch_shapes=[
            pltpu.VMEM((3, rows, depth), F32),
            pltpu.VMEM((2, depth, width), BF16),
            pltpu.VMEM((2, width, rank), BF16),
            pltpu.VMEM((depth, rank), F32),
            pltpu.VMEM((2, steps, rows, width), F32),
            pltpu.VMEM((2, steps, rows, width), F32),
            pltpu.VMEM((2, steps, rows, width), F32),
            pltpu.VMEM((2, rows, width), F32),
            pltpu.VMEM((rows, tokens), F32),
            pltpu.VMEM((tokens, rank), F32),
            pltpu.VMEM((2, slab, tokens), F32),
            pltpu.VMEM((2, slab, tokens), F32),
            pltpu.VMEM((2, slab, tokens), F32),
            pltpu.VMEM((2, slab, tokens), F32),
            pltpu.VMEM((3, strip, tokens), F32),
            dma((6,)), dma((6,)), dma((2,)), dma((2,)), dma((2,)), dma((2, steps)), dma((2,)),
            dma((2, steps * CUTS)), dma((steps,)),
            dma((2,)), dma((2,)), dma((2,)), dma((2,)), dma((3,)), dma((3,)), dma((2,)), dma((2,)),
            dma((2, 4)), dma((2, 4)), dma((2,)), dma((2,)),
        ],
        compiler_params=pltpu.CompilerParams(
            collective_id=2, has_side_effects=True, vmem_limit_bytes=60 * 2**20
        ),
        cost_estimate=pl.CostEstimate(
            flops=4 * tokens * depth * weight.shape[1],
            bytes_accessed=500 * 2**20,
            transcendentals=0,
        ),
    )(acts, weight, start)


TRI = ((0, 0), (1, 0), (1, 1), (2, 0), (2, 1), (2, 2))


def basis_kernel(
    blocks_ref, packed_ref, high_ref, low_ref, left_ref, right_ref, core_ref,
    grams, parts, square, pair_in, sum_in, whole, halves, tall, sent, landed, table,
    pair_send, pair_recv, sum_send, sum_recv, line_send, line_recv, tok_send, tok_recv, end_send, end_recv,
    *, features, columns,
):
    tok, row, z, core = place()
    _, tokens, rank = tall.shape
    width = blocks_ref.shape[2]
    third = tokens // 3
    piece = 6 * third // 16
    half = 8 * piece
    end = z // 2
    holds = (z == 0) | (z == 3)
    sibling = (tok, other(row, 1))
    toks = [tok, other(tok, 1), other(tok, 2), other(other(tok, 1), 2)]
    barrier = pltpu.get_barrier_semaphore()
    near = [sibling] + [(t, row) for t in toks[1:]] + [(tok, lax.rem(row + d, 8)) for d in (2, 4, 6)]
    for partner in near:
        pl.semaphore_signal(barrier, inc=1, device_id=partner, device_id_type=MESH)
    far = [(t, 6 - 2 * z + core) for t in toks[1:]]

    @pl.when(holds)
    def _():
        for partner in far:
            pl.semaphore_signal(barrier, inc=1, device_id=partner, device_id_type=MESH)

    pl.semaphore_wait(barrier, jnp.where(holds, 10, 7))

    mine = pl.ds(pl.multiple_of(core * half, 8), half)
    theirs = pl.ds(pl.multiple_of((1 - core) * half, 8), half)
    pair = remote(square.at[theirs], pair_in, pair_send.at[0], pair_recv.at[0], sibling)

    @pl.when(holds)
    def _():
        for at in range(2):
            first, second = split_two(blocks_ref[at])
            parts[0, at] = first
            parts[1, at] = second
        for n, (i, j) in enumerate(TRI):
            a, b = pl.ds(i * third, third), pl.ds(j * third, third)
            square[pl.ds(n * third, third), :] = sum(
                dots((parts[0, at, a], parts[1, at, a]), (parts[0, at, b], parts[1, at, b]), ((1,), (1,)))
                for at in range(2)
            )
        pair.start()

    quarter, strip = tokens // 16, tokens // 16 * rank // tokens
    for a in range(2):
        for b in range(2):
            for c in range(4):
                first, second = split_two(packed_ref[a, b, c, :quarter, :])
                at = pl.ds((4 * c + 2 * a + b) * quarter, quarter)
                grams[0, at, :] = first
                grams[1, at, :] = second
                for m in range(tokens // rank):
                    lines = pl.ds((8 * a + 4 * b + c) * quarter + m * strip, strip)
                    tall[1, lines, :] = (
                        packed_ref[a, b, c, quarter:, m * rank : (m + 1) * rank] / tokens
                    )
    gram_parts = (grams[0], grams[1])
    block = tall[1]
    tall[0] = dots(gram_parts, split_two(block), ((1,), (0,)))
    set_table(table, inner(block, tall[0]))

    def spot(to_core, to_tok, to_end):
        return pl.ds(pl.multiple_of(to_core * half + (to_tok * 2 + to_end) * piece, 8), piece)

    def sum_copy(d):
        to_tok = toks[d // 2]
        to_end = 1 - end if d % 2 else end
        return remote(
            square.at[spot(core, to_tok, to_end)], sum_in.at[d], sum_send.at[d], sum_recv.at[d],
            (to_tok, 6 * to_end + core),
        )

    @pl.when(holds)
    def _():
        pair.wait_recv()
        square[mine, :] = square[mine, :] + pair_in[...]
        for d in (7, 5, 3, 1, 6, 4, 2):
            sum_copy(d).start()

    factor_block(table, 0)
    factor_block(table, NB)

    here = spot(core, tok, end)

    def line_copy(i):
        to = (3 - i) + end * (2 * i - 3)
        return remote(whole.at[here], whole.at[here], line_send.at[i], line_recv.at[end], (tok, 2 * to + core))

    def tok_copy(source_end, d):
        place_of = spot(core, tok, source_end)
        return remote(
            whole.at[place_of], whole.at[place_of], tok_send.at[source_end, d], tok_recv.at[source_end, d],
            (toks[d], row),
        )

    @pl.when(holds)
    def _():
        total = square[here, :]
        for d in range(1, 8):
            sum_copy(d).wait_recv()
            total += sum_in[d]
        whole[here, :] = total
        for i in range(3):
            line_copy(i).start()
        for d in (3, 1, 2):
            tok_copy(end, d).start()

    factor_block(table, 2 * NB)
    for source in range(2):

        @pl.when(z != 3 * source)
        def _():
            landing = spot(core, tok, source)
            remote(
                whole.at[landing], whole.at[landing], line_send.at[0], line_recv.at[source], sibling
            ).wait_recv()
            for d in (3, 1, 2):
                tok_copy(source, d).start()

    factor_block(table, 3 * NB)
    tall[1] = outer(tall[0], table[:, rank:]) / tokens
    for source in range(2):
        for d in (1, 2, 3):
            landing = spot(core, toks[d], source)
            remote(
                whole.at[landing], whole.at[landing], tok_send.at[source, d], tok_recv.at[source, d], sibling
            ).wait_recv()
    last = remote(whole.at[mine], whole.at[mine], pair_send.at[1], pair_recv.at[1], sibling)
    last.start()
    remote(whole.at[theirs], whole.at[theirs], pair_send.at[1], pair_recv.at[1], sibling).wait_recv()
    first, second = split_two(whole[...])
    halves[0] = first
    halves[1] = second

    def squared(to, block):
        pieces = [split_two(block[i * third : (i + 1) * third, :]) for i in range(3)]
        for i in range(3):
            total = None
            for j in range(3):
                n = TRI.index((max(i, j), min(i, j)))
                at = pl.ds(n * third, third)
                dims = ((1,), (0,)) if i >= j else ((0,), (0,))
                term = dots((halves[0, at], halves[1, at]), pieces[j], dims)
                total = term if total is None else total + term
            tall[to, pl.ds(i * third, third), :] = total

    block = tall[1]
    squared(0, block)
    inverse = inverse_of(table, inner(block, tall[0]))
    tall[1] = outer(tall[0], inverse) / tokens

    block = tall[1]
    tall[0] = dots(gram_parts, split_two(block), ((1,), (0,)))
    inverse = inverse_of(table, inner(block, tall[0]))
    coef = split_two(outer(block, inverse))
    tall[1] = outer(tall[0], inverse) / tokens

    block = tall[1]
    ends = split_two(block)
    carry = remote(
        sent, landed, end_send.at[0], end_recv.at[0],
        (tok, jnp.where(z < 2, 2, 4) + core),
    )

    @pl.when(holds)
    def _():
        away = 1 - end
        sent[...] = dots((parts[0, away], parts[1, away]), ends, ((0,), (0,)))
        carry.start()
        landed[...] = dots((parts[0, end], parts[1, end]), ends, ((0,), (0,)))

    left_ref[...] = math.sqrt(features) * dots((high_ref[...], low_ref[...]), coef, ((0,), (0,)))
    squared(0, block)
    gram = inner(block, tall[0])
    inverse = inverse_of(table, gram)
    core_ref[...] = outer(gram, inverse)

    @pl.when(z == 1)
    def _():
        carry.wait_recv()

    @pl.when(z == 2)
    def _():
        carry.wait_recv()

    right_ref[...] = math.sqrt(columns) * outer(landed[...], inverse)

    @pl.when(holds)
    def _():
        carry.wait_send()
        pair.wait_send()
        for d in range(1, 8):
            sum_copy(d).wait_send()
        for i in range(3):
            line_copy(i).wait_send()

    for source in range(2):
        for d in (1, 2, 3):
            tok_copy(source, d).wait_send()
    last.wait_send()


def bases(blocks, packed, high, low, rank, features, columns):
    tokens = high.shape[0]
    width, depth = blocks.shape[2], high.shape[1]
    third = tokens // 3
    dma = pltpu.SemaphoreType.DMA
    return pl.pallas_call(
        functools.partial(basis_kernel, features=features, columns=columns),
        in_specs=[VMEM] * 4,
        out_specs=[VMEM] * 3,
        out_shape=[
            jax.ShapeDtypeStruct((depth, rank), F32),
            jax.ShapeDtypeStruct((width, rank), F32),
            jax.ShapeDtypeStruct((rank, rank), F32),
        ],
        scratch_shapes=[
            pltpu.VMEM((2, tokens, tokens), BF16),
            pltpu.VMEM((2, 2, tokens, width), BF16),
            pltpu.VMEM((6 * third, third), F32),
            pltpu.VMEM((3 * third, third), F32),
            pltpu.VMEM((8, 6 * third // 16, third), F32),
            pltpu.VMEM((6 * third, third), F32),
            pltpu.VMEM((2, 6 * third, third), BF16),
            pltpu.VMEM((2, tokens, rank), F32),
            pltpu.VMEM((width, rank), F32),
            pltpu.VMEM((width, rank), F32),
            pltpu.VMEM((rank, 2 * rank), F32),
            dma((2,)), dma((2,)), dma((8,)), dma((8,)), dma((3,)), dma((2,)),
            dma((2, 4)), dma((2, 4)), dma((1,)), dma((1,)),
        ],
        compiler_params=pltpu.CompilerParams(
            collective_id=3, has_side_effects=True, vmem_limit_bytes=56 * 2**20
        ),
    )(blocks, packed, high, low)


def token_space(hidden, resid, down_in, down_out, up_weight, start):
    features = up_weight.shape[0] * 8
    columns = up_weight.shape[1] * 4
    acts = activation_rows(hidden, resid, down_in, down_out)
    blocks, high, low, packed = applied_sums(acts, up_weight, start)
    return bases(blocks, packed, high, low, start.shape[1], features, columns)


def shards(hidden, *rest):
    tokens = hidden.shape[0] * lax.axis_size("tok")
    if tokens > 1024 or (lax.axis_size("tok"), lax.axis_size("row")) != (4, 8):
        return feature_space(hidden, *rest)
    return token_space(hidden, *rest)


def solution(mesh):
    placed = (
        P("tok", "row"),
        P("tok", "row"),
        P("row", None),
        P(None, "row"),
        P("row", "tok"),
        P("tok", None),
    )
    return jax.shard_map(
        shards,
        mesh=mesh,
        in_specs=placed,
        out_specs=(P("row", None), P(("tok", "row"), None), P()),
        check_vma=False,
    )
```

```python
import functools
import math

import jax
import jax.numpy as jnp
from jax import lax
from jax.experimental import pallas as pl
from jax.experimental.pallas import tpu as pltpu
from jax.sharding import PartitionSpec as P

ITERS = 2
HIGH = lax.Precision.HIGHEST
F32 = jnp.float32
BF16 = jnp.bfloat16


def inner(first, second):
    return lax.dot_general(
        first, second, (((0,), (0,)), ((), ())), precision=HIGH, preferred_element_type=F32
    )


def outer(first, second):
    return lax.dot_general(
        first, second, (((1,), (1,)), ((), ())), precision=HIGH, preferred_element_type=F32
    )


def solve_lower(lower, block):
    return jax.scipy.linalg.solve_triangular(lower, block.T, lower=True).T


def activations(hidden, resid, down_in, down_out):
    partial_value = jnp.dot(hidden, down_in, preferred_element_type=F32)
    code = lax.psum(partial_value, "row")
    return resid.astype(F32) + jnp.dot(code, down_out.astype(F32), precision=HIGH)


def feature_space(hidden, resid, down_in, down_out, up_weight, start):
    act_full = activations(hidden, resid, down_in, down_out)
    total_tokens = act_full.shape[0] * lax.axis_size("tok")
    features = up_weight.shape[0] * lax.axis_size("row")
    columns = up_weight.shape[1] * lax.axis_size("tok")

    def whiten(block):
        applied = lax.psum(jnp.dot(act_full, block, precision=HIGH), "row")
        return lax.psum(inner(act_full, applied), "tok") / total_tokens

    weight = up_weight.astype(F32)
    right = start.astype(F32)
    for step in range(ITERS):
        image = lax.psum(jnp.dot(weight, right, precision=HIGH), "tok")
        target = whiten(image)
        lower = jnp.linalg.cholesky(lax.psum(inner(target, target), "row"))
        left = solve_lower(lower, target)
        back = whiten(left)
        share = lax.psum_scatter(inner(weight, back), "row", scatter_dimension=0, tiled=True)
        right_lower = jnp.linalg.cholesky(lax.psum(inner(share, share), ("tok", "row")))
        piece = solve_lower(right_lower, share)
        right = lax.all_gather(piece, "row", axis=0, tiled=True)
    core = lax.psum(inner(back, jnp.dot(weight, right, precision=HIGH)), ("tok", "row"))
    return (math.sqrt(features) * left, math.sqrt(columns) * piece, core)


def dots(first, second, dims):
    def one(x, y):
        return lax.dot_general(x, y, (dims, ((), ())), preferred_element_type=F32)

    return one(first[1], second[0]) + one(first[0], second[1]) + one(first[0], second[0])


NB = 64


def factor_block(table, at):
    size = table.shape[0]
    eye = (
        lax.broadcasted_iota(jnp.int32, (NB, NB), 0) == lax.broadcasted_iota(jnp.int32, (NB, NB), 1)
    ).astype(F32)
    back = (
        lax.broadcasted_iota(jnp.int32, (NB, NB), 0) == lax.broadcasted_iota(jnp.int32, (NB, NB), 1) + 1
    ).astype(F32)
    index = lax.broadcasted_iota(jnp.int32, (8, 2 * NB), 0)
    work = jnp.concatenate([table[at : at + NB, at : at + NB], eye], axis=1)
    groups = [work[k : k + 8, :] for k in range(0, NB, 8)]
    wide = (8, 2 * NB)
    for j in range(0, NB, 2):
        own, spot = divmod(j, 8)
        ones = [jnp.broadcast_to(groups[k][:, j : j + 1], wide) for k in range(own, NB // 8)]
        twos = [jnp.broadcast_to(groups[k][:, j + 1 : j + 2], wide) for k in range(own, NB // 8)]
        row1, row2 = groups[own][spot : spot + 1, :], groups[own][spot + 1 : spot + 2, :]
        a, b = ones[0][spot : spot + 1, :], twos[0][spot : spot + 1, :]
        d = twos[0][spot + 1 : spot + 2, :]
        inverse = 1.0 / (a * d - b * b)
        first = (d * row1 - b * row2) * inverse
        second = (a * row2 - b * row1) * inverse
        for k in range(own, NB // 8):
            change = ones[k - own] * first + twos[k - own] * second
            if k == own:
                change = jnp.where(index > spot + 1, change, 0.0)
            groups[k] = groups[k] - change
    work = jnp.concatenate(groups, axis=0)
    odd = lax.rem(lax.broadcasted_iota(jnp.int32, (NB, 1), 0), 2) == 1
    pivot = jnp.sum(work[:, :NB] * eye, axis=1, keepdims=True)
    cross = jnp.sum(work[:, :NB] * back, axis=1, keepdims=True)
    right = work[:, NB:]
    before = jnp.concatenate([right[:1], right[:-1]], axis=0)
    ratio = jnp.where(odd, cross / jnp.concatenate([pivot[:1], pivot[:-1]], axis=0), 0.0)
    small = (right - ratio * before) * lax.rsqrt(pivot - ratio * cross)
    rows = jnp.dot(small, table[at : at + NB, :], precision=HIGH, preferred_element_type=F32)
    table[at : at + NB, :] = rows
    if at + NB < size:
        below = rows[:, at + NB : size]
        table[at + NB :, :] = table[at + NB :, :] - inner(below, rows)


def set_table(table, gram):
    size = gram.shape[0]
    table[:, :size] = gram
    table[:, size:] = (
        lax.broadcasted_iota(jnp.int32, (size, size), 0)
        == lax.broadcasted_iota(jnp.int32, (size, size), 1)
    ).astype(F32)


def inverse_of(table, gram):
    set_table(table, gram)
    for at in range(0, gram.shape[0], NB):
        factor_block(table, at)
    return table[:, gram.shape[0] :]


MESH = pl.DeviceIdType.MESH
VMEM = pl.BlockSpec(memory_space=pltpu.VMEM)
ANY = pl.BlockSpec(memory_space=pl.ANY)


def place():
    tok, row = lax.axis_index("tok"), lax.axis_index("row")
    return tok, row, row // 2, lax.rem(row, 2)


def other(index, bit):
    if bit == 1:
        return index + 1 - 2 * lax.rem(index, 2)
    return lax.rem(index + 2, 4)


def greet(partners):
    barrier = pltpu.get_barrier_semaphore()
    for partner in partners:
        pl.semaphore_signal(barrier, inc=1, device_id=partner, device_id_type=MESH)
    pl.semaphore_wait(barrier, len(partners))


def remote(src, dst, send_sem, recv_sem, partner):
    return pltpu.make_async_remote_copy(
        src_ref=src, dst_ref=dst, send_sem=send_sem, recv_sem=recv_sem,
        device_id=partner, device_id_type=MESH,
    )


def split_two(block):
    first = block.astype(BF16)
    return first, (block - first.astype(F32)).astype(BF16)


def split_three(block):
    first, rest = block.astype(BF16), None
    rest = block - first.astype(F32)
    second = rest.astype(BF16)
    third = (rest - second.astype(F32)).astype(BF16)
    return first, second, third


def acts_kernel(
    hidden_ref, resid_ref, din_ref, dout_ref, acts_ref,
    part, inbox, code, sum_send, sum_recv, code_send, code_recv,
):
    tok, row, _, _ = place()
    share = hidden_ref.shape[0] // 8
    peers = [(tok, lax.rem(row + d, 8)) for d in range(1, 8)]
    greet(peers)

    part[...] = jnp.dot(hidden_ref[...], din_ref[...], preferred_element_type=F32)
    copies = []
    for d, peer in enumerate(peers):
        piece = part.at[pl.ds(pl.multiple_of(peer[1] * share, 8), share)]
        copies.append(remote(piece, inbox.at[d], sum_send.at[d], sum_recv.at[d], peer))
        copies[-1].start()
    mine = pl.ds(pl.multiple_of(row * share, 8), share)
    total = part[mine, :]
    for d in range(7):
        copies[d].wait_recv()
        total += inbox[d]
    code[mine, :] = total
    gathers = []
    for d, peer in enumerate(peers):
        gathers.append(remote(code.at[mine], code.at[mine], code_send.at[d], code_recv.at[d], peer))
        gathers[-1].start()
    for d in range(7):
        source = pl.ds(pl.multiple_of(lax.rem(row + 7 - d, 8) * share, 8), share)
        remote(code.at[source], code.at[source], code_send.at[d], code_recv.at[d], peers[d]).wait_recv()
    first, second, third = split_three(code[...])
    weight = dout_ref[...]
    own = jnp.dot(third, weight, preferred_element_type=F32)
    own += jnp.dot(second, weight, preferred_element_type=F32)
    own += jnp.dot(first, weight, preferred_element_type=F32)
    acts_ref[...] = resid_ref[...].astype(F32) + own
    for copy in copies + gathers:
        copy.wait_send()


def activation_rows(hidden, resid, down_in, down_out):
    rows, width = resid.shape
    rank = down_in.shape[1]
    dma = pltpu.SemaphoreType.DMA
    return pl.pallas_call(
        acts_kernel,
        in_specs=[VMEM] * 4,
        out_specs=VMEM,
        out_shape=jax.ShapeDtypeStruct((rows, width), F32),
        scratch_shapes=[
            pltpu.VMEM((rows, rank), F32),
            pltpu.VMEM((7, rows // 8, rank), F32),
            pltpu.VMEM((rows, rank), F32),
            dma((7,)), dma((7,)), dma((7,)), dma((7,)),
        ],
        compiler_params=pltpu.CompilerParams(
            collective_id=1, has_side_effects=True, vmem_limit_bytes=24 * 2**20
        ),
    )(hidden, resid, down_in, down_out)


CUTS = 8
LAG = 4


DIAGONAL = 16
FIRST = 23
HOP = 5
STEP = 4
SHARE = 56


def applied_kernel(
    own_ref, weight_ref, start_ref, out_ref, high_ref, low_ref, packed_ref,
    base, held, begin, image, own, inner_in, line_in, stage,
    gp, xp, own_x, inner_x, line_x, stage_x, x_in,
    move_send, move_recv, weight_sem, begin_sem, pair_send, pair_recv, line_send, line_recv, out_sem,
    xp_send, xp_recv, xl_send, xl_recv, xs_send, xs_recv, bc_send, bc_recv, tk_send, tk_recv, last_send, last_recv,
):
    tok, row, z, core = place()
    rows = own_ref.shape[0]
    _, steps, _, width = own.shape
    tokens = 4 * rows
    rank = begin.shape[2]
    cut = rows // CUTS
    quarter, strip = rows // 4, rows // 4 * rank // tokens
    sibling = (tok, other(row, 1))
    toks = [tok, other(tok, 1), other(tok, 2), other(other(tok, 1), 2)]
    by_x, by_y = (toks[1], row), (toks[2], row)
    down, up = (tok, row - 2), (tok, row + 2)
    barrier = pltpu.get_barrier_semaphore()
    for partner in [sibling] + [(t, row) for t in toks[1:]]:
        pl.semaphore_signal(barrier, inc=1, device_id=partner, device_id_type=MESH)

    @pl.when(z > 0)
    def _():
        pl.semaphore_signal(barrier, inc=1, device_id=down, device_id_type=MESH)

    @pl.when(z < 3)
    def _():
        pl.semaphore_signal(barrier, inc=1, device_id=up, device_id_type=MESH)

    pl.semaphore_wait(barrier, jnp.where((z == 0) | (z == 3), 5, 6))

    def block_of(step, which):
        side = core if which // 2 else 1 - core
        return 4 * (which % 2) + 2 * lax.rem(step, 2) + side

    def load(step, which):
        columns = pl.ds(pl.multiple_of(block_of(step, which) * width, 128), width)
        return pltpu.make_async_copy(weight_ref.at[:, columns], held.at[which % 2], weight_sem.at[which % 2])

    def load_begin(step, which):
        lines = pl.ds(pl.multiple_of(block_of(step, which) * width, 16), width)
        return pltpu.make_async_copy(start_ref.at[lines], begin.at[which % 2], begin_sem.at[which % 2])

    for which in range(2):
        load(0, which).start()

    half = rows // 2
    top, bottom = pl.ds(0, half), pl.ds(half, half)

    def move(index):
        source, to, piece, partner = (
            (own_ref, 0, top, by_x),
            (own_ref, 1, bottom, by_y),
            (own_ref, 0, bottom, by_x),
            (own_ref, 1, top, by_y),
            (base.at[0], 2, top, by_y),
            (base.at[1], 2, bottom, by_x),
        )[index]
        return remote(
            source.at[piece], base.at[to, piece], move_send.at[index], move_recv.at[index], partner
        )

    for index in range(4):
        move(index).start()

    def emit(value, group):
        at = pl.ds(pl.multiple_of(group * rows, 16), rows)
        first, second = split_two(value)
        high_ref[at, :] = first
        low_ref[at, :] = second

    emit(own_ref[...], tok)
    image[...] = jnp.zeros_like(image)

    def group_of(step):
        slot = step // 2
        across = lax.rem(lax.rem(tok, 2) + lax.rem(slot, 2), 2)
        return 2 * lax.rem(tok // 2 + slot // 2, 2) + across

    def pair_copy(step, end):
        return remote(
            stage.at[end], inner_in.at[end, step], pair_send.at[end], pair_recv.at[end, step], sibling
        )

    def line_copy(end, step, piece, at):
        part = pl.ds(pl.multiple_of(piece * cut, 8), cut)
        return remote(
            own.at[end, step, part], line_in.at[end, step, part], line_send.at[end],
            line_recv.at[end, at], down if end == 0 else up,
        )

    def out_copy(end, step):
        part = pl.ds(pl.multiple_of(group_of(step) * rows, 8), rows)
        return pltpu.make_async_copy(own.at[end, step], out_ref.at[lax.rem(step, 2), part], out_sem.at[step])

    def multiply(step, which):
        part = pl.ds(pl.multiple_of(group_of(step) * rows, 16), rows)
        end = which % 2
        load(step, which).wait()
        weight = held[which % 2]
        value = jnp.dot(low_ref[part, :], weight, preferred_element_type=F32)
        value += jnp.dot(high_ref[part, :], weight, preferred_element_type=F32)
        if which < 2:

            @pl.when(step >= 1)
            def _():
                pair_copy(step - 1, end).wait_send()

            stage[end] = value
            pair_copy(step, end).start()
        else:
            own[end, step] = value

        @pl.when((step >= 1) & (step < 3))
        def _():
            load_begin(step, which).wait()
            image[...] = image[...] + jnp.dot(
                held[which % 2], begin[which % 2], preferred_element_type=F32
            )

        following, next_which = (step, which + 2) if which < 2 else (step + 1, which - 2)

        @pl.when(following < steps)
        def _():
            load(following, next_which).start()

        @pl.when((following >= 1) & (following < 3))
        def _():
            load_begin(following, next_which).start()

    hops_of = [3 - z, z]

    def forward(end, at):
        hops = hops_of[end]
        at = at - LAG * hops

        @pl.when((at >= 0) & (at < CUTS * steps))
        def _():
            step, piece = at // CUTS, lax.rem(at, CUTS)
            part = pl.ds(pl.multiple_of(piece * cut, 8), cut)

            @pl.when(piece == 0)
            def _():
                pair_copy(step, end).wait_recv()

            own[end, step, part, :] = own[end, step, part, :] + inner_in[end, step, part, :]

            @pl.when(hops > 0)
            def _():
                line_copy(end, step, piece, at).wait_recv()
                own[end, step, part, :] = own[end, step, part, :] + line_in[end, step, part, :]

            @pl.when(hops < 3)
            def _():
                line_copy(end, step, piece, at).start()

            @pl.when((hops == 3) & (piece == CUTS - 1))
            def _():
                out_copy(end, step).start()

    def x_pair(end):
        return remote(stage_x.at[end], inner_x.at[end], xp_send.at[end], xp_recv.at[end], sibling)

    def x_line(end):
        return remote(
            own_x.at[end], line_x.at[end], xl_send.at[end], xl_recv.at[end], down if end == 0 else up
        )

    def x_sum(d):
        piece = pl.ds(pl.multiple_of(rows * toks[d], 8), rows)
        return remote(xp.at[piece], x_in.at[d - 1], xs_send.at[d - 1], xs_recv.at[d - 1], (toks[d], row))

    def spread(end):
        piece = packed_ref.at[end, core, tok]
        return remote(piece, piece, bc_send.at[end], bc_recv.at[end], up if end == 0 else down)

    def token_spread(end, d):
        piece = packed_ref.at[end, core, tok]
        return remote(piece, piece, tk_send.at[end, d], tk_recv.at[end, d], (toks[d], row))

    def token_landing(end, d):
        piece = packed_ref.at[end, core, toks[d]]
        return remote(piece, piece, tk_send.at[end, d], tk_recv.at[end, d], (toks[d], row))

    def last_copy(end, side):
        piece = packed_ref.at[end, side]
        return remote(piece, piece, last_send.at[end], last_recv.at[end], sibling)

    def x_fill():
        mine = pl.ds(pl.multiple_of(rows * tok, 8), rows)
        total = xp[mine, :]
        for d in (1, 2, 3):
            x_sum(d).wait_recv()
            total += x_in[d - 1]
        xp[mine, :] = total
        for end in range(2):
            for target, side in ((own_x, core), (stage_x, 1 - core)):
                place_of = 2 * end + side
                at = pl.ds(pl.multiple_of(place_of * quarter, 8), quarter)
                target[end, :quarter, :] = gp[at, :]
                for m in range(tokens // rank):
                    lines = pl.ds(pl.multiple_of(tok * rows + place_of * quarter + m * strip, 8), strip)
                    target[end, quarter:, m * rank : (m + 1) * rank] = xp[lines, :]
            x_pair(end).start()

    def small(step, piece):
        def on(when, extra, action):
            when = when * CUTS // 8
            if piece == when % CUTS:
                pl.when((step == when // CUTS) & extra)(action)

        def arrive_first():
            for index in (0, 1):
                move(index).wait_recv()
                move(4 + index).start()

        def arrive_x():
            move(2).wait_recv()
            emit(base[0], toks[1])

        def arrive_y():
            move(3).wait_recv()
            emit(base[1], toks[2])

        def arrive_diagonal():
            move(4).wait_recv()
            move(5).wait_recv()
            emit(base[2], toks[3])

        def gram():
            mine = pl.ds(pl.multiple_of(tok * rows, 16), rows)
            gp[...] = dots((high_ref[mine, :], low_ref[mine, :]), (high_ref[...], low_ref[...]), ((1,), (1,)))

        def imaged():
            xp[...] = dots((high_ref[...], low_ref[...]), split_two(image[...]), ((1,), (0,)))
            for d in (3, 1, 2):
                x_sum(d).start()

        always = step >= 0
        on(4, always, arrive_first)
        on(7, always, arrive_x)
        on(12, always, arrive_y)
        on(DIAGONAL, always, arrive_diagonal)
        on(DIAGONAL + 1, always, imaged)
        on(DIAGONAL + 2, always, gram)
        on(FIRST - 2, always, x_fill)
        for end in range(2):
            hops = hops_of[end]

            def joined(end=end):
                x_pair(end).wait_recv()
                own_x[end] = own_x[end] + inner_x[end]

            on(FIRST, always, joined)

            def passed(end=end):
                x_line(end).wait_recv()
                own_x[end] = own_x[end] + line_x[end]

            def passed_on(end=end):
                passed(end)
                x_line(end).start()

            on(FIRST, hops == 0, lambda end=end: x_line(end).start())
            on(FIRST + HOP, hops == 1, passed_on)
            on(FIRST + 2 * HOP, hops == 2, passed_on)

            def to_tokens(end=end):
                for d in (3, 1, 2):
                    token_spread(end, d).start()

            def packed(end=end):
                passed(end)
                packed_ref[end, core, tok] = own_x[end]
                spread(end).start()
                to_tokens(end)

            def relay(end=end):
                spread(end).wait_recv()
                spread(end).start()
                to_tokens(end)

            def relay_end(end=end):
                spread(end).wait_recv()
                to_tokens(end)

            on(FIRST + 3 * HOP, hops == 3, packed)
            on(FIRST + 3 * HOP + STEP, hops == 2, relay)
            on(FIRST + 3 * HOP + 2 * STEP, hops == 1, relay)
            on(FIRST + 3 * HOP + 3 * STEP, hops == 0, relay_end)

        def share_out():
            for end in range(2):
                for d in (1, 2, 3):
                    token_landing(end, d).wait_recv()
                last_copy(end, core).start()

        on(SHARE, always, share_out)

    for which in range(4):
        multiply(0, which)

    def one(step, carry):
        for piece in range(CUTS):
            for which in range(4):
                if piece == which * CUTS // 4:

                    @pl.when(step + 1 < steps)
                    def _():
                        multiply(step + 1, which)

            for end in range(2):
                forward(end, step * CUTS + piece)
            small(step, piece)
        return carry

    lax.fori_loop(0, steps + -(-3 * LAG // CUTS), one, 0)

    for index in range(6):
        move(index).wait_send()
    for d in (1, 2, 3):
        x_sum(d).wait_send()
    for end in range(2):
        hops = hops_of[end]
        last_copy(end, 1 - core).wait_recv()
        last_copy(end, core).wait_send()
        x_pair(end).wait_send()
        for d in (1, 2, 3):
            token_spread(end, d).wait_send()
        pair_copy(steps - 1, end).wait_send()

        @pl.when(hops < 3)
        def _():
            x_line(end).wait_send()
            remote(
                own.at[end], line_in.at[end], line_send.at[end], line_recv.at[end, 0],
                down if end == 0 else up,
            ).wait_send()

        @pl.when(hops > 0)
        def _():
            spread(end).wait_send()

        @pl.when(hops == 3)
        def _():
            for step in range(steps):
                out_copy(end, step).wait()


def applied_sums(acts, weight, start):
    rows, depth = acts.shape
    tokens = 4 * rows
    width = weight.shape[1] // 8
    rank = start.shape[1]
    steps = 8
    quarter = rows // 4
    strip = quarter * rank // tokens
    slab = quarter + strip
    dma = pltpu.SemaphoreType.DMA
    return pl.pallas_call(
        applied_kernel,
        in_specs=[VMEM, ANY, ANY],
        out_specs=[ANY, VMEM, VMEM, VMEM],
        out_shape=[
            jax.ShapeDtypeStruct((2, tokens, width), F32),
            jax.ShapeDtypeStruct((tokens, depth), BF16),
            jax.ShapeDtypeStruct((tokens, depth), BF16),
            jax.ShapeDtypeStruct((2, 2, 4, quarter + strip, tokens), F32),
        ],
        scratch_shapes=[
            pltpu.VMEM((3, rows, depth), F32),
            pltpu.VMEM((2, depth, width), BF16),
            pltpu.VMEM((2, width, rank), BF16),
            pltpu.VMEM((depth, rank), F32),
            pltpu.VMEM((2, steps, rows, width), F32),
            pltpu.VMEM((2, steps, rows, width), F32),
            pltpu.VMEM((2, steps, rows, width), F32),
            pltpu.VMEM((2, rows, width), F32),
            pltpu.VMEM((rows, tokens), F32),
            pltpu.VMEM((tokens, rank), F32),
            pltpu.VMEM((2, slab, tokens), F32),
            pltpu.VMEM((2, slab, tokens), F32),
            pltpu.VMEM((2, slab, tokens), F32),
            pltpu.VMEM((2, slab, tokens), F32),
            pltpu.VMEM((3, rows, rank), F32),
            dma((6,)), dma((6,)), dma((2,)), dma((2,)), dma((2,)), dma((2, steps)), dma((2,)),
            dma((2, steps * CUTS)), dma((steps,)),
            dma((2,)), dma((2,)), dma((2,)), dma((2,)), dma((3,)), dma((3,)), dma((2,)), dma((2,)),
            dma((2, 4)), dma((2, 4)), dma((2,)), dma((2,)),
        ],
        compiler_params=pltpu.CompilerParams(
            collective_id=2, has_side_effects=True, vmem_limit_bytes=60 * 2**20
        ),
        cost_estimate=pl.CostEstimate(
            flops=4 * tokens * depth * weight.shape[1],
            bytes_accessed=500 * 2**20,
            transcendentals=0,
        ),
    )(acts, weight, start)


TRI = ((0, 0), (1, 0), (1, 1), (2, 0), (2, 1), (2, 2))


def basis_kernel(
    blocks_ref, packed_ref, high_ref, low_ref, left_ref, right_ref, core_ref,
    grams, parts, square, pair_in, sum_in, whole, halves, tall, sent, landed, table,
    pair_send, pair_recv, sum_send, sum_recv, line_send, line_recv, tok_send, tok_recv, end_send, end_recv,
    *, features, columns,
):
    tok, row, z, core = place()
    _, tokens, rank = tall.shape
    width = blocks_ref.shape[2]
    third = tokens // 3
    piece = 6 * third // 16
    half = 8 * piece
    end = z // 2
    holds = (z == 0) | (z == 3)
    sibling = (tok, other(row, 1))
    toks = [tok, other(tok, 1), other(tok, 2), other(other(tok, 1), 2)]
    barrier = pltpu.get_barrier_semaphore()
    near = [sibling] + [(t, row) for t in toks[1:]] + [(tok, lax.rem(row + d, 8)) for d in (2, 4, 6)]
    for partner in near:
        pl.semaphore_signal(barrier, inc=1, device_id=partner, device_id_type=MESH)
    far = [(t, 6 - 2 * z + core) for t in toks[1:]]

    @pl.when(holds)
    def _():
        for partner in far:
            pl.semaphore_signal(barrier, inc=1, device_id=partner, device_id_type=MESH)

    pl.semaphore_wait(barrier, jnp.where(holds, 10, 7))

    mine = pl.ds(pl.multiple_of(core * half, 8), half)
    theirs = pl.ds(pl.multiple_of((1 - core) * half, 8), half)
    pair = remote(square.at[theirs], pair_in, pair_send.at[0], pair_recv.at[0], sibling)

    @pl.when(holds)
    def _():
        for at in range(2):
            first, second = split_two(blocks_ref[at])
            parts[0, at] = first
            parts[1, at] = second
        for n, (i, j) in enumerate(TRI):
            a, b = pl.ds(i * third, third), pl.ds(j * third, third)
            square[pl.ds(n * third, third), :] = sum(
                dots((parts[0, at, a], parts[1, at, a]), (parts[0, at, b], parts[1, at, b]), ((1,), (1,)))
                for at in range(2)
            )
        pair.start()

    quarter, strip = tokens // 16, tokens // 16 * rank // tokens
    for a in range(2):
        for b in range(2):
            for c in range(4):
                first, second = split_two(packed_ref[a, b, c, :quarter, :])
                at = pl.ds((4 * c + 2 * a + b) * quarter, quarter)
                grams[0, at, :] = first
                grams[1, at, :] = second
                for m in range(tokens // rank):
                    lines = pl.ds((4 * c + 2 * a + b) * quarter + m * strip, strip)
                    tall[1, lines, :] = (
                        packed_ref[a, b, c, quarter:, m * rank : (m + 1) * rank] / tokens
                    )
    gram_parts = (grams[0], grams[1])
    block = tall[1]
    tall[0] = dots(gram_parts, split_two(block), ((1,), (0,)))
    set_table(table, inner(block, tall[0]))

    def spot(to_core, to_tok, to_end):
        return pl.ds(pl.multiple_of(to_core * half + (to_tok * 2 + to_end) * piece, 8), piece)

    def sum_copy(d):
        to_tok = toks[d // 2]
        to_end = 1 - end if d % 2 else end
        return remote(
            square.at[spot(core, to_tok, to_end)], sum_in.at[d], sum_send.at[d], sum_recv.at[d],
            (to_tok, 6 * to_end + core),
        )

    @pl.when(holds)
    def _():
        pair.wait_recv()
        square[mine, :] = square[mine, :] + pair_in[...]
        for d in (7, 5, 3, 1, 6, 4, 2):
            sum_copy(d).start()

    factor_block(table, 0)
    factor_block(table, NB)

    here = spot(core, tok, end)

    def line_copy(i):
        to = (3 - i) + end * (2 * i - 3)
        return remote(whole.at[here], whole.at[here], line_send.at[i], line_recv.at[end], (tok, 2 * to + core))

    def tok_copy(source_end, d):
        place_of = spot(core, tok, source_end)
        return remote(
            whole.at[place_of], whole.at[place_of], tok_send.at[source_end, d], tok_recv.at[source_end, d],
            (toks[d], row),
        )

    @pl.when(holds)
    def _():
        total = square[here, :]
        for d in range(1, 8):
            sum_copy(d).wait_recv()
            total += sum_in[d]
        whole[here, :] = total
        for i in range(3):
            line_copy(i).start()
        for d in (3, 1, 2):
            tok_copy(end, d).start()

    factor_block(table, 2 * NB)
    for source in range(2):

        @pl.when(z != 3 * source)
        def _():
            landing = spot(core, tok, source)
            remote(
                whole.at[landing], whole.at[landing], line_send.at[0], line_recv.at[source], sibling
            ).wait_recv()
            for d in (3, 1, 2):
                tok_copy(source, d).start()

    factor_block(table, 3 * NB)
    tall[1] = outer(tall[0], table[:, rank:]) / tokens
    for source in range(2):
        for d in (1, 2, 3):
            landing = spot(core, toks[d], source)
            remote(
                whole.at[landing], whole.at[landing], tok_send.at[source, d], tok_recv.at[source, d], sibling
            ).wait_recv()
    last = remote(whole.at[mine], whole.at[mine], pair_send.at[1], pair_recv.at[1], sibling)
    last.start()
    remote(whole.at[theirs], whole.at[theirs], pair_send.at[1], pair_recv.at[1], sibling).wait_recv()
    first, second = split_two(whole[...])
    halves[0] = first
    halves[1] = second

    def squared(to, block):
        pieces = [split_two(block[i * third : (i + 1) * third, :]) for i in range(3)]
        for i in range(3):
            total = None
            for j in range(3):
                n = TRI.index((max(i, j), min(i, j)))
                at = pl.ds(n * third, third)
                dims = ((1,), (0,)) if i >= j else ((0,), (0,))
                term = dots((halves[0, at], halves[1, at]), pieces[j], dims)
                total = term if total is None else total + term
            tall[to, pl.ds(i * third, third), :] = total

    block = tall[1]
    squared(0, block)
    inverse = inverse_of(table, inner(block, tall[0]))
    tall[1] = outer(tall[0], inverse) / tokens

    block = tall[1]
    tall[0] = dots(gram_parts, split_two(block), ((1,), (0,)))
    inverse = inverse_of(table, inner(block, tall[0]))
    coef = split_two(outer(block, inverse))
    tall[1] = outer(tall[0], inverse) / tokens

    block = tall[1]
    ends = split_two(block)
    carry = remote(
        sent, landed, end_send.at[0], end_recv.at[0],
        (tok, jnp.where(z < 2, 2, 4) + core),
    )

    @pl.when(holds)
    def _():
        away = 1 - end
        sent[...] = dots((parts[0, away], parts[1, away]), ends, ((0,), (0,)))
        carry.start()
        landed[...] = dots((parts[0, end], parts[1, end]), ends, ((0,), (0,)))

    left_ref[...] = math.sqrt(features) * dots((high_ref[...], low_ref[...]), coef, ((0,), (0,)))
    squared(0, block)
    gram = inner(block, tall[0])
    inverse = inverse_of(table, gram)
    core_ref[...] = outer(gram, inverse)

    @pl.when(z == 1)
    def _():
        carry.wait_recv()

    @pl.when(z == 2)
    def _():
        carry.wait_recv()

    right_ref[...] = math.sqrt(columns) * outer(landed[...], inverse)

    @pl.when(holds)
    def _():
        carry.wait_send()
        pair.wait_send()
        for d in range(1, 8):
            sum_copy(d).wait_send()
        for i in range(3):
            line_copy(i).wait_send()

    for source in range(2):
        for d in (1, 2, 3):
            tok_copy(source, d).wait_send()
    last.wait_send()


def bases(blocks, packed, high, low, rank, features, columns):
    tokens = high.shape[0]
    width, depth = blocks.shape[2], high.shape[1]
    third = tokens // 3
    dma = pltpu.SemaphoreType.DMA
    return pl.pallas_call(
        functools.partial(basis_kernel, features=features, columns=columns),
        in_specs=[VMEM] * 4,
        out_specs=[VMEM] * 3,
        out_shape=[
            jax.ShapeDtypeStruct((depth, rank), F32),
            jax.ShapeDtypeStruct((width, rank), F32),
            jax.ShapeDtypeStruct((rank, rank), F32),
        ],
        scratch_shapes=[
            pltpu.VMEM((2, tokens, tokens), BF16),
            pltpu.VMEM((2, 2, tokens, width), BF16),
            pltpu.VMEM((6 * third, third), F32),
            pltpu.VMEM((3 * third, third), F32),
            pltpu.VMEM((8, 6 * third // 16, third), F32),
            pltpu.VMEM((6 * third, third), F32),
            pltpu.VMEM((2, 6 * third, third), BF16),
            pltpu.VMEM((2, tokens, rank), F32),
            pltpu.VMEM((width, rank), F32),
            pltpu.VMEM((width, rank), F32),
            pltpu.VMEM((rank, 2 * rank), F32),
            dma((2,)), dma((2,)), dma((8,)), dma((8,)), dma((3,)), dma((2,)),
            dma((2, 4)), dma((2, 4)), dma((1,)), dma((1,)),
        ],
        compiler_params=pltpu.CompilerParams(
            collective_id=3, has_side_effects=True, vmem_limit_bytes=56 * 2**20
        ),
    )(blocks, packed, high, low)


def token_space(hidden, resid, down_in, down_out, up_weight, start):
    features = up_weight.shape[0] * 8
    columns = up_weight.shape[1] * 4
    acts = activation_rows(hidden, resid, down_in, down_out)
    blocks, high, low, packed = applied_sums(acts, up_weight, start)
    return bases(blocks, packed, high, low, start.shape[1], features, columns)


def shards(hidden, *rest):
    tokens = hidden.shape[0] * lax.axis_size("tok")
    if tokens > 1024 or (lax.axis_size("tok"), lax.axis_size("row")) != (4, 8):
        return feature_space(hidden, *rest)
    return token_space(hidden, *rest)


def solution(mesh):
    placed = (
        P("tok", "row"),
        P("tok", "row"),
        P("row", None),
        P(None, "row"),
        P("row", "tok"),
        P("tok", None),
    )
    return jax.shard_map(
        shards,
        mesh=mesh,
        in_specs=placed,
        out_specs=(P("row", None), P(("tok", "row"), None), P()),
        check_vma=False,
    )
```

```python
import functools
import math

import jax
import jax.numpy as jnp
from jax import lax
from jax.experimental import pallas as pl
from jax.experimental.pallas import tpu as pltpu
from jax.sharding import PartitionSpec as P

ITERS = 2
HIGH = lax.Precision.HIGHEST
F32 = jnp.float32
BF16 = jnp.bfloat16


def inner(first, second):
    return lax.dot_general(
        first, second, (((0,), (0,)), ((), ())), precision=HIGH, preferred_element_type=F32
    )


def outer(first, second):
    return lax.dot_general(
        first, second, (((1,), (1,)), ((), ())), precision=HIGH, preferred_element_type=F32
    )


def solve_lower(lower, block):
    return jax.scipy.linalg.solve_triangular(lower, block.T, lower=True).T


def activations(hidden, resid, down_in, down_out):
    partial_value = jnp.dot(hidden, down_in, preferred_element_type=F32)
    code = lax.psum(partial_value, "row")
    return resid.astype(F32) + jnp.dot(code, down_out.astype(F32), precision=HIGH)


def feature_space(hidden, resid, down_in, down_out, up_weight, start):
    act_full = activations(hidden, resid, down_in, down_out)
    total_tokens = act_full.shape[0] * lax.axis_size("tok")
    features = up_weight.shape[0] * lax.axis_size("row")
    columns = up_weight.shape[1] * lax.axis_size("tok")

    def whiten(block):
        applied = lax.psum(jnp.dot(act_full, block, precision=HIGH), "row")
        return lax.psum(inner(act_full, applied), "tok") / total_tokens

    weight = up_weight.astype(F32)
    right = start.astype(F32)
    for step in range(ITERS):
        image = lax.psum(jnp.dot(weight, right, precision=HIGH), "tok")
        target = whiten(image)
        lower = jnp.linalg.cholesky(lax.psum(inner(target, target), "row"))
        left = solve_lower(lower, target)
        back = whiten(left)
        share = lax.psum_scatter(inner(weight, back), "row", scatter_dimension=0, tiled=True)
        right_lower = jnp.linalg.cholesky(lax.psum(inner(share, share), ("tok", "row")))
        piece = solve_lower(right_lower, share)
        right = lax.all_gather(piece, "row", axis=0, tiled=True)
    core = lax.psum(inner(back, jnp.dot(weight, right, precision=HIGH)), ("tok", "row"))
    return (math.sqrt(features) * left, math.sqrt(columns) * piece, core)


def dots(first, second, dims):
    def one(x, y):
        return lax.dot_general(x, y, (dims, ((), ())), preferred_element_type=F32)

    return one(first[1], second[0]) + one(first[0], second[1]) + one(first[0], second[0])


def turned(first, second):
    return dots(split_two(first), split_two(second), ((1,), (1,)))


NB = 64


def factor_block(table, at):
    size = table.shape[0]
    eye = (
        lax.broadcasted_iota(jnp.int32, (NB, NB), 0) == lax.broadcasted_iota(jnp.int32, (NB, NB), 1)
    ).astype(F32)
    back = (
        lax.broadcasted_iota(jnp.int32, (NB, NB), 0) == lax.broadcasted_iota(jnp.int32, (NB, NB), 1) + 1
    ).astype(F32)
    index = lax.broadcasted_iota(jnp.int32, (8, 2 * NB), 0)
    work = jnp.concatenate([table[at : at + NB, at : at + NB], eye], axis=1)
    groups = [work[k : k + 8, :] for k in range(0, NB, 8)]
    wide = (8, 2 * NB)
    for j in range(0, NB, 2):
        own, spot = divmod(j, 8)
        ones = [jnp.broadcast_to(groups[k][:, j : j + 1], wide) for k in range(own, NB // 8)]
        twos = [jnp.broadcast_to(groups[k][:, j + 1 : j + 2], wide) for k in range(own, NB // 8)]
        row1, row2 = groups[own][spot : spot + 1, :], groups[own][spot + 1 : spot + 2, :]
        a, b = ones[0][spot : spot + 1, :], twos[0][spot : spot + 1, :]
        d = twos[0][spot + 1 : spot + 2, :]
        inverse = 1.0 / (a * d - b * b)
        first = (d * row1 - b * row2) * inverse
        second = (a * row2 - b * row1) * inverse
        for k in range(own, NB // 8):
            change = ones[k - own] * first + twos[k - own] * second
            if k == own:
                change = jnp.where(index > spot + 1, change, 0.0)
            groups[k] = groups[k] - change
    work = jnp.concatenate(groups, axis=0)
    odd = lax.rem(lax.broadcasted_iota(jnp.int32, (NB, 1), 0), 2) == 1
    pivot = jnp.sum(work[:, :NB] * eye, axis=1, keepdims=True)
    cross = jnp.sum(work[:, :NB] * back, axis=1, keepdims=True)
    right = work[:, NB:]
    before = jnp.concatenate([right[:1], right[:-1]], axis=0)
    ratio = jnp.where(odd, cross / jnp.concatenate([pivot[:1], pivot[:-1]], axis=0), 0.0)
    small = (right - ratio * before) * lax.rsqrt(pivot - ratio * cross)
    rows = jnp.dot(small, table[at : at + NB, :], precision=HIGH, preferred_element_type=F32)
    table[at : at + NB, :] = rows
    if at + NB < size:
        below = rows[:, at + NB : size]
        table[at + NB :, :] = table[at + NB :, :] - inner(below, rows)


def set_table(table, gram):
    size = gram.shape[0]
    table[:, :size] = gram
    table[:, size:] = (
        lax.broadcasted_iota(jnp.int32, (size, size), 0)
        == lax.broadcasted_iota(jnp.int32, (size, size), 1)
    ).astype(F32)


def inverse_of(table, gram):
    set_table(table, gram)
    for at in range(0, gram.shape[0], NB):
        factor_block(table, at)
    return table[:, gram.shape[0] :]


MESH = pl.DeviceIdType.MESH
VMEM = pl.BlockSpec(memory_space=pltpu.VMEM)
ANY = pl.BlockSpec(memory_space=pl.ANY)


def place():
    tok, row = lax.axis_index("tok"), lax.axis_index("row")
    return tok, row, row // 2, lax.rem(row, 2)


def other(index, bit):
    if bit == 1:
        return index + 1 - 2 * lax.rem(index, 2)
    return lax.rem(index + 2, 4)


def greet(partners):
    barrier = pltpu.get_barrier_semaphore()
    for partner in partners:
        pl.semaphore_signal(barrier, inc=1, device_id=partner, device_id_type=MESH)
    pl.semaphore_wait(barrier, len(partners))


def remote(src, dst, send_sem, recv_sem, partner):
    return pltpu.make_async_remote_copy(
        src_ref=src, dst_ref=dst, send_sem=send_sem, recv_sem=recv_sem,
        device_id=partner, device_id_type=MESH,
    )


def split_two(block):
    first = block.astype(BF16)
    return first, (block - first.astype(F32)).astype(BF16)


def split_three(block):
    first, rest = block.astype(BF16), None
    rest = block - first.astype(F32)
    second = rest.astype(BF16)
    third = (rest - second.astype(F32)).astype(BF16)
    return first, second, third


def acts_kernel(
    hidden_hbm, resid_hbm, din_hbm, dout_hbm, acts_ref,
    hidden_ref, resid_ref, din_ref, dout_ref,
    part, inbox, code, load_sem, sum_send, sum_recv, code_send, code_recv,
):
    tok, row, _, _ = place()
    loads = [
        pltpu.make_async_copy(source, target, load_sem.at[i])
        for i, (source, target) in enumerate(
            (
                (din_hbm, din_ref),
                (hidden_hbm, hidden_ref),
                (dout_hbm, dout_ref),
                (resid_hbm, resid_ref),
            )
        )
    ]
    for load in loads:
        load.start()
    share = hidden_ref.shape[0] // 8
    peers = [(tok, lax.rem(row + d, 8)) for d in range(1, 8)]
    greet(peers)

    loads[0].wait()
    loads[1].wait()
    part[...] = jnp.dot(hidden_ref[...], din_ref[...], preferred_element_type=F32)
    copies = []
    for d, peer in enumerate(peers):
        piece = part.at[pl.ds(pl.multiple_of(peer[1] * share, 8), share)]
        copies.append(remote(piece, inbox.at[d], sum_send.at[d], sum_recv.at[d], peer))
        copies[-1].start()
    mine = pl.ds(pl.multiple_of(row * share, 8), share)
    total = part[mine, :]
    for d in range(7):
        copies[d].wait_recv()
        total += inbox[d]
    code[mine, :] = total
    gathers = []
    for d, peer in enumerate(peers):
        gathers.append(remote(code.at[mine], code.at[mine], code_send.at[d], code_recv.at[d], peer))
        gathers[-1].start()
    for d in range(7):
        source = pl.ds(pl.multiple_of(lax.rem(row + 7 - d, 8) * share, 8), share)
        remote(code.at[source], code.at[source], code_send.at[d], code_recv.at[d], peers[d]).wait_recv()
    loads[2].wait()
    loads[3].wait()
    first, second, third = split_three(code[...])
    weight = dout_ref[...]
    own = jnp.dot(third, weight, preferred_element_type=F32)
    own += jnp.dot(second, weight, preferred_element_type=F32)
    own += jnp.dot(first, weight, preferred_element_type=F32)
    acts_ref[...] = resid_ref[...].astype(F32) + own
    for copy in copies + gathers:
        copy.wait_send()


def activation_rows(hidden, resid, down_in, down_out):
    rows, width = resid.shape
    rank = down_in.shape[1]
    dma = pltpu.SemaphoreType.DMA
    return pl.pallas_call(
        acts_kernel,
        in_specs=[ANY] * 4,
        out_specs=VMEM,
        out_shape=jax.ShapeDtypeStruct((rows, width), F32),
        scratch_shapes=[
            pltpu.VMEM(hidden.shape, BF16),
            pltpu.VMEM(resid.shape, BF16),
            pltpu.VMEM(down_in.shape, BF16),
            pltpu.VMEM(down_out.shape, BF16),
            pltpu.VMEM((rows, rank), F32),
            pltpu.VMEM((7, rows // 8, rank), F32),
            pltpu.VMEM((rows, rank), F32),
            dma((4,)), dma((7,)), dma((7,)), dma((7,)), dma((7,)),
        ],
        compiler_params=pltpu.CompilerParams(
            collective_id=1, has_side_effects=True, vmem_limit_bytes=60 * 2**20
        ),
    )(hidden, resid, down_in, down_out)


CUTS = 8
LAG = 4


DIAGONAL = 16
FIRST = 23
HOP = 5
STEP = 4
SHARE = 56


def applied_kernel(
    own_ref, weight_ref, start_ref, out_ref, high_ref, low_ref, packed_ref,
    base, held, begin, image, own, inner_in, line_in, stage,
    gp, xp, own_x, inner_x, line_x, stage_x, x_in,
    move_send, move_recv, weight_sem, begin_sem, pair_send, pair_recv, line_send, line_recv, out_sem,
    xp_send, xp_recv, xl_send, xl_recv, xs_send, xs_recv, bc_send, bc_recv, tk_send, tk_recv, last_send, last_recv,
):
    tok, row, z, core = place()
    rows = own_ref.shape[0]
    _, steps, _, width = own.shape
    tokens = 4 * rows
    rank = begin.shape[2]
    cut = rows // CUTS
    quarter, strip = rows // 4, rows // 4 * rank // tokens
    sibling = (tok, other(row, 1))
    toks = [tok, other(tok, 1), other(tok, 2), other(other(tok, 1), 2)]
    by_x, by_y = (toks[1], row), (toks[2], row)
    down, up = (tok, row - 2), (tok, row + 2)
    barrier = pltpu.get_barrier_semaphore()
    for partner in [sibling] + [(t, row) for t in toks[1:]]:
        pl.semaphore_signal(barrier, inc=1, device_id=partner, device_id_type=MESH)

    @pl.when(z > 0)
    def _():
        pl.semaphore_signal(barrier, inc=1, device_id=down, device_id_type=MESH)

    @pl.when(z < 3)
    def _():
        pl.semaphore_signal(barrier, inc=1, device_id=up, device_id_type=MESH)

    pl.semaphore_wait(barrier, jnp.where((z == 0) | (z == 3), 5, 6))

    def block_of(step, which):
        side = core if which // 2 else 1 - core
        return 4 * (which % 2) + 2 * lax.rem(step, 2) + side

    def load(step, which):
        columns = pl.ds(pl.multiple_of(block_of(step, which) * width, 128), width)
        return pltpu.make_async_copy(weight_ref.at[:, columns], held.at[which % 2], weight_sem.at[which % 2])

    def load_begin(step, which):
        lines = pl.ds(pl.multiple_of(block_of(step, which) * width, 16), width)
        return pltpu.make_async_copy(start_ref.at[lines], begin.at[which % 2], begin_sem.at[which % 2])

    for which in range(2):
        load(0, which).start()

    half = rows // 2
    top, bottom = pl.ds(0, half), pl.ds(half, half)

    def move(index):
        source, to, piece, partner = (
            (own_ref, 0, top, by_x),
            (own_ref, 1, bottom, by_y),
            (own_ref, 0, bottom, by_x),
            (own_ref, 1, top, by_y),
            (base.at[0], 2, top, by_y),
            (base.at[1], 2, bottom, by_x),
        )[index]
        return remote(
            source.at[piece], base.at[to, piece], move_send.at[index], move_recv.at[index], partner
        )

    for index in range(4):
        move(index).start()

    def emit(value, group):
        at = pl.ds(pl.multiple_of(group * rows, 16), rows)
        first, second = split_two(value)
        high_ref[at, :] = first
        low_ref[at, :] = second

    emit(own_ref[...], tok)
    image[...] = jnp.zeros_like(image)

    def group_of(step):
        slot = step // 2
        across = lax.rem(lax.rem(tok, 2) + lax.rem(slot, 2), 2)
        return 2 * lax.rem(tok // 2 + slot // 2, 2) + across

    def pair_copy(step, end):
        return remote(
            stage.at[end], inner_in.at[end, step], pair_send.at[end], pair_recv.at[end, step], sibling
        )

    def line_copy(end, step, piece, at):
        part = pl.ds(pl.multiple_of(piece * cut, 8), cut)
        return remote(
            own.at[end, step, part], line_in.at[end, step, part], line_send.at[end],
            line_recv.at[end, at], down if end == 0 else up,
        )

    def out_copy(end, step):
        part = pl.ds(pl.multiple_of(group_of(step) * rows, 8), rows)
        return pltpu.make_async_copy(own.at[end, step], out_ref.at[lax.rem(step, 2), part], out_sem.at[step])

    def multiply(step, which):
        part = pl.ds(pl.multiple_of(group_of(step) * rows, 16), rows)
        end = which % 2
        load(step, which).wait()
        weight = held[which % 2]
        value = jnp.dot(low_ref[part, :], weight, preferred_element_type=F32)
        value += jnp.dot(high_ref[part, :], weight, preferred_element_type=F32)
        if which < 2:

            @pl.when(step >= 1)
            def _():
                pair_copy(step - 1, end).wait_send()

            stage[end] = value
            pair_copy(step, end).start()
        else:
            own[end, step] = value

        @pl.when((step >= 1) & (step < 3))
        def _():
            load_begin(step, which).wait()
            image[...] = image[...] + jnp.dot(
                held[which % 2], begin[which % 2], preferred_element_type=F32
            )

        following, next_which = (step, which + 2) if which < 2 else (step + 1, which - 2)

        @pl.when(following < steps)
        def _():
            load(following, next_which).start()

        @pl.when((following >= 1) & (following < 3))
        def _():
            load_begin(following, next_which).start()

    hops_of = [3 - z, z]

    def forward(end, at):
        hops = hops_of[end]
        at = at - LAG * hops

        @pl.when((at >= 0) & (at < CUTS * steps))
        def _():
            step, piece = at // CUTS, lax.rem(at, CUTS)
            part = pl.ds(pl.multiple_of(piece * cut, 8), cut)

            @pl.when(piece == 0)
            def _():
                pair_copy(step, end).wait_recv()

            own[end, step, part, :] = own[end, step, part, :] + inner_in[end, step, part, :]

            @pl.when(hops > 0)
            def _():
                line_copy(end, step, piece, at).wait_recv()
                own[end, step, part, :] = own[end, step, part, :] + line_in[end, step, part, :]

            @pl.when(hops < 3)
            def _():
                line_copy(end, step, piece, at).start()

            @pl.when((hops == 3) & (piece == CUTS - 1))
            def _():
                out_copy(end, step).start()

    def x_pair(end):
        return remote(stage_x.at[end], inner_x.at[end], xp_send.at[end], xp_recv.at[end], sibling)

    def x_line(end):
        return remote(
            own_x.at[end], line_x.at[end], xl_send.at[end], xl_recv.at[end], down if end == 0 else up
        )

    def x_sum(d):
        piece = pl.ds(pl.multiple_of(rows * toks[d], 8), rows)
        return remote(xp.at[piece], x_in.at[d - 1], xs_send.at[d - 1], xs_recv.at[d - 1], (toks[d], row))

    def spread(end):
        piece = packed_ref.at[end, core, tok]
        return remote(piece, piece, bc_send.at[end], bc_recv.at[end], up if end == 0 else down)

    def token_spread(end, d):
        piece = packed_ref.at[end, core, tok]
        return remote(piece, piece, tk_send.at[end, d], tk_recv.at[end, d], (toks[d], row))

    def token_landing(end, d):
        piece = packed_ref.at[end, core, toks[d]]
        return remote(piece, piece, tk_send.at[end, d], tk_recv.at[end, d], (toks[d], row))

    def last_copy(end, side):
        piece = packed_ref.at[end, side]
        return remote(piece, piece, last_send.at[end], last_recv.at[end], sibling)

    def x_fill():
        mine = pl.ds(pl.multiple_of(rows * tok, 8), rows)
        total = xp[mine, :]
        for d in (1, 2, 3):
            x_sum(d).wait_recv()
            total += x_in[d - 1]
        xp[mine, :] = total
        for end in range(2):
            for target, side in ((own_x, core), (stage_x, 1 - core)):
                place_of = 2 * end + side
                at = pl.ds(pl.multiple_of(place_of * quarter, 8), quarter)
                target[end, :quarter, :] = gp[at, :]
                for m in range(tokens // rank):
                    lines = pl.ds(pl.multiple_of(tok * rows + place_of * quarter + m * strip, 8), strip)
                    target[end, quarter:, m * rank : (m + 1) * rank] = xp[lines, :]
            x_pair(end).start()

    def small(step, piece):
        def on(when, extra, action):
            when = when * CUTS // 8
            if piece == when % CUTS:
                pl.when((step == when // CUTS) & extra)(action)

        def arrive_first():
            for index in (0, 1):
                move(index).wait_recv()
                move(4 + index).start()

        def arrive_x():
            move(2).wait_recv()
            emit(base[0], toks[1])

        def arrive_y():
            move(3).wait_recv()
            emit(base[1], toks[2])

        def arrive_diagonal():
            move(4).wait_recv()
            move(5).wait_recv()
            emit(base[2], toks[3])

        def gram():
            mine = pl.ds(pl.multiple_of(tok * rows, 16), rows)
            gp[...] = dots((high_ref[mine, :], low_ref[mine, :]), (high_ref[...], low_ref[...]), ((1,), (1,)))

        def imaged():
            xp[...] = dots((high_ref[...], low_ref[...]), split_two(image[...]), ((1,), (0,)))
            for d in (3, 1, 2):
                x_sum(d).start()

        always = step >= 0
        on(4, always, arrive_first)
        on(7, always, arrive_x)
        on(12, always, arrive_y)
        on(DIAGONAL, always, arrive_diagonal)
        on(DIAGONAL + 1, always, imaged)
        on(DIAGONAL + 2, always, gram)
        on(FIRST - 2, always, x_fill)
        for end in range(2):
            hops = hops_of[end]

            def joined(end=end):
                x_pair(end).wait_recv()
                own_x[end] = own_x[end] + inner_x[end]

            on(FIRST, always, joined)

            def passed(end=end):
                x_line(end).wait_recv()
                own_x[end] = own_x[end] + line_x[end]

            def passed_on(end=end):
                passed(end)
                x_line(end).start()

            on(FIRST, hops == 0, lambda end=end: x_line(end).start())
            on(FIRST + HOP, hops == 1, passed_on)
            on(FIRST + 2 * HOP, hops == 2, passed_on)

            def to_tokens(end=end):
                for d in (3, 1, 2):
                    token_spread(end, d).start()

            def packed(end=end):
                passed(end)
                packed_ref[end, core, tok] = own_x[end]
                spread(end).start()
                to_tokens(end)

            def relay(end=end):
                spread(end).wait_recv()
                spread(end).start()
                to_tokens(end)

            def relay_end(end=end):
                spread(end).wait_recv()
                to_tokens(end)

            on(FIRST + 3 * HOP, hops == 3, packed)
            on(FIRST + 3 * HOP + STEP, hops == 2, relay)
            on(FIRST + 3 * HOP + 2 * STEP, hops == 1, relay)
            on(FIRST + 3 * HOP + 3 * STEP, hops == 0, relay_end)

        def share_out():
            for end in range(2):
                for d in (1, 2, 3):
                    token_landing(end, d).wait_recv()
                last_copy(end, core).start()

        on(SHARE, always, share_out)

    for which in range(4):
        multiply(0, which)

    def one(step, carry):
        for piece in range(CUTS):
            for which in range(4):
                if piece == which * CUTS // 4:

                    @pl.when(step + 1 < steps)
                    def _():
                        multiply(step + 1, which)

            for end in range(2):
                forward(end, step * CUTS + piece)
            small(step, piece)
        return carry

    lax.fori_loop(0, steps + -(-3 * LAG // CUTS), one, 0)

    for index in range(6):
        move(index).wait_send()
    for d in (1, 2, 3):
        x_sum(d).wait_send()
    for end in range(2):
        hops = hops_of[end]
        last_copy(end, 1 - core).wait_recv()
        last_copy(end, core).wait_send()
        x_pair(end).wait_send()
        for d in (1, 2, 3):
            token_spread(end, d).wait_send()
        pair_copy(steps - 1, end).wait_send()

        @pl.when(hops < 3)
        def _():
            x_line(end).wait_send()
            remote(
                own.at[end], line_in.at[end], line_send.at[end], line_recv.at[end, 0],
                down if end == 0 else up,
            ).wait_send()

        @pl.when(hops > 0)
        def _():
            spread(end).wait_send()

        @pl.when(hops == 3)
        def _():
            for step in range(steps):
                out_copy(end, step).wait()


def applied_sums(acts, weight, start):
    rows, depth = acts.shape
    tokens = 4 * rows
    width = weight.shape[1] // 8
    rank = start.shape[1]
    steps = 8
    quarter = rows // 4
    strip = quarter * rank // tokens
    slab = quarter + strip
    dma = pltpu.SemaphoreType.DMA
    return pl.pallas_call(
        applied_kernel,
        in_specs=[VMEM, ANY, ANY],
        out_specs=[ANY, VMEM, VMEM, VMEM],
        out_shape=[
            jax.ShapeDtypeStruct((2, tokens, width), F32),
            jax.ShapeDtypeStruct((tokens, depth), BF16),
            jax.ShapeDtypeStruct((tokens, depth), BF16),
            jax.ShapeDtypeStruct((2, 2, 4, quarter + strip, tokens), F32),
        ],
        scratch_shapes=[
            pltpu.VMEM((3, rows, depth), F32),
            pltpu.VMEM((2, depth, width), BF16),
            pltpu.VMEM((2, width, rank), BF16),
            pltpu.VMEM((depth, rank), F32),
            pltpu.VMEM((2, steps, rows, width), F32),
            pltpu.VMEM((2, steps, rows, width), F32),
            pltpu.VMEM((2, steps, rows, width), F32),
            pltpu.VMEM((2, rows, width), F32),
            pltpu.VMEM((rows, tokens), F32),
            pltpu.VMEM((tokens, rank), F32),
            pltpu.VMEM((2, slab, tokens), F32),
            pltpu.VMEM((2, slab, tokens), F32),
            pltpu.VMEM((2, slab, tokens), F32),
            pltpu.VMEM((2, slab, tokens), F32),
            pltpu.VMEM((3, rows, rank), F32),
            dma((6,)), dma((6,)), dma((2,)), dma((2,)), dma((2,)), dma((2, steps)), dma((2,)),
            dma((2, steps * CUTS)), dma((steps,)),
            dma((2,)), dma((2,)), dma((2,)), dma((2,)), dma((3,)), dma((3,)), dma((2,)), dma((2,)),
            dma((2, 4)), dma((2, 4)), dma((2,)), dma((2,)),
        ],
        compiler_params=pltpu.CompilerParams(
            collective_id=2, has_side_effects=True, vmem_limit_bytes=60 * 2**20
        ),
        cost_estimate=pl.CostEstimate(
            flops=4 * tokens * depth * weight.shape[1],
            bytes_accessed=500 * 2**20,
            transcendentals=0,
        ),
    )(acts, weight, start)


TRI = ((0, 0), (1, 0), (1, 1), (2, 0), (2, 1), (2, 2))


def basis_kernel(
    blocks_ref, packed_ref, high_ref, low_ref, left_ref, right_ref, core_ref,
    grams, parts, square, pair_in, sum_in, whole, halves, tall, sent, landed, table,
    pair_send, pair_recv, sum_send, sum_recv, line_send, line_recv, tok_send, tok_recv, end_send, end_recv,
    *, features, columns,
):
    tok, row, z, core = place()
    _, tokens, rank = tall.shape
    width = blocks_ref.shape[2]
    third = tokens // 3
    piece = 6 * third // 16
    half = 8 * piece
    end = z // 2
    holds = (z == 0) | (z == 3)
    sibling = (tok, other(row, 1))
    toks = [tok, other(tok, 1), other(tok, 2), other(other(tok, 1), 2)]
    barrier = pltpu.get_barrier_semaphore()
    near = [sibling] + [(t, row) for t in toks[1:]] + [(tok, lax.rem(row + d, 8)) for d in (2, 4, 6)]
    for partner in near:
        pl.semaphore_signal(barrier, inc=1, device_id=partner, device_id_type=MESH)
    far = [(t, 6 - 2 * z + core) for t in toks[1:]]

    @pl.when(holds)
    def _():
        for partner in far:
            pl.semaphore_signal(barrier, inc=1, device_id=partner, device_id_type=MESH)

    pl.semaphore_wait(barrier, jnp.where(holds, 10, 7))

    mine = pl.ds(pl.multiple_of(core * half, 8), half)
    theirs = pl.ds(pl.multiple_of((1 - core) * half, 8), half)
    pair = remote(square.at[theirs], pair_in, pair_send.at[0], pair_recv.at[0], sibling)

    @pl.when(holds)
    def _():
        for at in range(2):
            first, second = split_two(blocks_ref[at])
            parts[0, at] = first
            parts[1, at] = second
        for n, (i, j) in enumerate(TRI):
            a, b = pl.ds(i * third, third), pl.ds(j * third, third)
            square[pl.ds(n * third, third), :] = sum(
                dots((parts[0, at, a], parts[1, at, a]), (parts[0, at, b], parts[1, at, b]), ((1,), (1,)))
                for at in range(2)
            )
        pair.start()

    quarter, strip = tokens // 16, tokens // 16 * rank // tokens
    for a in range(2):
        for b in range(2):
            for c in range(4):
                first, second = split_two(packed_ref[a, b, c, :quarter, :])
                at = pl.ds((4 * c + 2 * a + b) * quarter, quarter)
                grams[0, at, :] = first
                grams[1, at, :] = second
                for m in range(tokens // rank):
                    lines = pl.ds((4 * c + 2 * a + b) * quarter + m * strip, strip)
                    tall[1, lines, :] = (
                        packed_ref[a, b, c, quarter:, m * rank : (m + 1) * rank] / tokens
                    )
    gram_parts = (grams[0], grams[1])
    block = tall[1]
    tall[0] = dots(gram_parts, split_two(block), ((1,), (0,)))
    set_table(table, inner(block, tall[0]))

    def spot(to_core, to_tok, to_end):
        return pl.ds(pl.multiple_of(to_core * half + (to_tok * 2 + to_end) * piece, 8), piece)

    def sum_copy(d):
        to_tok = toks[d // 2]
        to_end = 1 - end if d % 2 else end
        return remote(
            square.at[spot(core, to_tok, to_end)], sum_in.at[d], sum_send.at[d], sum_recv.at[d],
            (to_tok, 6 * to_end + core),
        )

    @pl.when(holds)
    def _():
        pair.wait_recv()
        square[mine, :] = square[mine, :] + pair_in[...]
        for d in (7, 5, 3, 1, 6, 4, 2):
            sum_copy(d).start()

    factor_block(table, 0)
    factor_block(table, NB)

    here = spot(core, tok, end)

    def line_copy(i):
        to = (3 - i) + end * (2 * i - 3)
        return remote(whole.at[here], whole.at[here], line_send.at[i], line_recv.at[end], (tok, 2 * to + core))

    def tok_copy(source_end, d):
        place_of = spot(core, tok, source_end)
        return remote(
            whole.at[place_of], whole.at[place_of], tok_send.at[source_end, d], tok_recv.at[source_end, d],
            (toks[d], row),
        )

    @pl.when(holds)
    def _():
        total = square[here, :]
        for d in range(1, 8):
            sum_copy(d).wait_recv()
            total += sum_in[d]
        whole[here, :] = total
        for i in range(3):
            line_copy(i).start()
        for d in (3, 1, 2):
            tok_copy(end, d).start()

    factor_block(table, 2 * NB)
    for source in range(2):

        @pl.when(z != 3 * source)
        def _():
            landing = spot(core, tok, source)
            remote(
                whole.at[landing], whole.at[landing], line_send.at[0], line_recv.at[source], sibling
            ).wait_recv()
            for d in (3, 1, 2):
                tok_copy(source, d).start()

    factor_block(table, 3 * NB)
    tall[1] = turned(tall[0], table[:, rank:]) / tokens
    for source in range(2):
        for d in (1, 2, 3):
            landing = spot(core, toks[d], source)
            remote(
                whole.at[landing], whole.at[landing], tok_send.at[source, d], tok_recv.at[source, d], sibling
            ).wait_recv()
    last = remote(whole.at[mine], whole.at[mine], pair_send.at[1], pair_recv.at[1], sibling)
    last.start()
    remote(whole.at[theirs], whole.at[theirs], pair_send.at[1], pair_recv.at[1], sibling).wait_recv()
    first, second = split_two(whole[...])
    halves[0] = first
    halves[1] = second

    def squared(to, block):
        pieces = [split_two(block[i * third : (i + 1) * third, :]) for i in range(3)]
        for i in range(3):
            total = None
            for j in range(3):
                n = TRI.index((max(i, j), min(i, j)))
                at = pl.ds(n * third, third)
                dims = ((1,), (0,)) if i >= j else ((0,), (0,))
                term = dots((halves[0, at], halves[1, at]), pieces[j], dims)
                total = term if total is None else total + term
            tall[to, pl.ds(i * third, third), :] = total

    block = tall[1]
    squared(0, block)
    inverse = inverse_of(table, inner(block, tall[0]))
    tall[1] = turned(tall[0], inverse) / tokens

    block = tall[1]
    tall[0] = dots(gram_parts, split_two(block), ((1,), (0,)))
    inverse = inverse_of(table, inner(block, tall[0]))
    coef = split_two(turned(block, inverse))
    tall[1] = turned(tall[0], inverse) / tokens

    block = tall[1]
    ends = split_two(block)
    carry = remote(
        sent, landed, end_send.at[0], end_recv.at[0],
        (tok, jnp.where(z < 2, 2, 4) + core),
    )

    @pl.when(holds)
    def _():
        away = 1 - end
        sent[...] = dots((parts[0, away], parts[1, away]), ends, ((0,), (0,)))
        carry.start()
        landed[...] = dots((parts[0, end], parts[1, end]), ends, ((0,), (0,)))

    left_ref[...] = math.sqrt(features) * dots((high_ref[...], low_ref[...]), coef, ((0,), (0,)))
    squared(0, block)
    gram = inner(block, tall[0])
    inverse = inverse_of(table, gram)
    core_ref[...] = outer(gram, inverse)

    @pl.when(z == 1)
    def _():
        carry.wait_recv()

    @pl.when(z == 2)
    def _():
        carry.wait_recv()

    right_ref[...] = math.sqrt(columns) * turned(landed[...], inverse)

    @pl.when(holds)
    def _():
        carry.wait_send()
        pair.wait_send()
        for d in range(1, 8):
            sum_copy(d).wait_send()
        for i in range(3):
            line_copy(i).wait_send()

    for source in range(2):
        for d in (1, 2, 3):
            tok_copy(source, d).wait_send()
    last.wait_send()


def bases(blocks, packed, high, low, rank, features, columns):
    tokens = high.shape[0]
    width, depth = blocks.shape[2], high.shape[1]
    third = tokens // 3
    dma = pltpu.SemaphoreType.DMA
    return pl.pallas_call(
        functools.partial(basis_kernel, features=features, columns=columns),
        in_specs=[VMEM] * 4,
        out_specs=[VMEM] * 3,
        out_shape=[
            jax.ShapeDtypeStruct((depth, rank), F32),
            jax.ShapeDtypeStruct((width, rank), F32),
            jax.ShapeDtypeStruct((rank, rank), F32),
        ],
        scratch_shapes=[
            pltpu.VMEM((2, tokens, tokens), BF16),
            pltpu.VMEM((2, 2, tokens, width), BF16),
            pltpu.VMEM((6 * third, third), F32),
            pltpu.VMEM((3 * third, third), F32),
            pltpu.VMEM((8, 6 * third // 16, third), F32),
            pltpu.VMEM((6 * third, third), F32),
            pltpu.VMEM((2, 6 * third, third), BF16),
            pltpu.VMEM((2, tokens, rank), F32),
            pltpu.VMEM((width, rank), F32),
            pltpu.VMEM((width, rank), F32),
            pltpu.VMEM((rank, 2 * rank), F32),
            dma((2,)), dma((2,)), dma((8,)), dma((8,)), dma((3,)), dma((2,)),
            dma((2, 4)), dma((2, 4)), dma((1,)), dma((1,)),
        ],
        compiler_params=pltpu.CompilerParams(
            collective_id=3, has_side_effects=True, vmem_limit_bytes=56 * 2**20
        ),
    )(blocks, packed, high, low)


def token_space(hidden, resid, down_in, down_out, up_weight, start):
    features = up_weight.shape[0] * 8
    columns = up_weight.shape[1] * 4
    acts = activation_rows(hidden, resid, down_in, down_out)
    blocks, high, low, packed = applied_sums(acts, up_weight, start)
    return bases(blocks, packed, high, low, start.shape[1], features, columns)


def shards(hidden, *rest):
    tokens = hidden.shape[0] * lax.axis_size("tok")
    if tokens > 1024 or (lax.axis_size("tok"), lax.axis_size("row")) != (4, 8):
        return feature_space(hidden, *rest)
    return token_space(hidden, *rest)


def solution(mesh):
    placed = (
        P("tok", "row"),
        P("tok", "row"),
        P("row", None),
        P(None, "row"),
        P("row", "tok"),
        P("tok", None),
    )
    return jax.shard_map(
        shards,
        mesh=mesh,
        in_specs=placed,
        out_specs=(P("row", None), P(("tok", "row"), None), P()),
        check_vma=False,
    )
```

```python
import functools
import math

import jax
import jax.numpy as jnp
from jax import lax
from jax.experimental import pallas as pl
from jax.experimental.pallas import tpu as pltpu
from jax.sharding import PartitionSpec as P

ITERS = 2
HIGH = lax.Precision.HIGHEST
F32 = jnp.float32
BF16 = jnp.bfloat16


def inner(first, second):
    return lax.dot_general(
        first, second, (((0,), (0,)), ((), ())), precision=HIGH, preferred_element_type=F32
    )


def outer(first, second):
    return lax.dot_general(
        first, second, (((1,), (1,)), ((), ())), precision=HIGH, preferred_element_type=F32
    )


def solve_lower(lower, block):
    return jax.scipy.linalg.solve_triangular(lower, block.T, lower=True).T


def activations(hidden, resid, down_in, down_out):
    partial_value = jnp.dot(hidden, down_in, preferred_element_type=F32)
    code = lax.psum(partial_value, "row")
    return resid.astype(F32) + jnp.dot(code, down_out.astype(F32), precision=HIGH)


def feature_space(hidden, resid, down_in, down_out, up_weight, start):
    act_full = activations(hidden, resid, down_in, down_out)
    total_tokens = act_full.shape[0] * lax.axis_size("tok")
    features = up_weight.shape[0] * lax.axis_size("row")
    columns = up_weight.shape[1] * lax.axis_size("tok")

    def whiten(block):
        applied = lax.psum(jnp.dot(act_full, block, precision=HIGH), "row")
        return lax.psum(inner(act_full, applied), "tok") / total_tokens

    weight = up_weight.astype(F32)
    right = start.astype(F32)
    for step in range(ITERS):
        image = lax.psum(jnp.dot(weight, right, precision=HIGH), "tok")
        target = whiten(image)
        lower = jnp.linalg.cholesky(lax.psum(inner(target, target), "row"))
        left = solve_lower(lower, target)
        back = whiten(left)
        share = lax.psum_scatter(inner(weight, back), "row", scatter_dimension=0, tiled=True)
        right_lower = jnp.linalg.cholesky(lax.psum(inner(share, share), ("tok", "row")))
        piece = solve_lower(right_lower, share)
        right = lax.all_gather(piece, "row", axis=0, tiled=True)
    core = lax.psum(inner(back, jnp.dot(weight, right, precision=HIGH)), ("tok", "row"))
    return (math.sqrt(features) * left, math.sqrt(columns) * piece, core)


def dots(first, second, dims):
    def one(x, y):
        return lax.dot_general(x, y, (dims, ((), ())), preferred_element_type=F32)

    return one(first[1], second[0]) + one(first[0], second[1]) + one(first[0], second[0])


def turned(first, second):
    return dots(split_two(first), split_two(second), ((1,), (1,)))


NB = 64


def factor_block(table, at):
    size = table.shape[0]
    eye = (
        lax.broadcasted_iota(jnp.int32, (NB, NB), 0) == lax.broadcasted_iota(jnp.int32, (NB, NB), 1)
    ).astype(F32)
    back = (
        lax.broadcasted_iota(jnp.int32, (NB, NB), 0) == lax.broadcasted_iota(jnp.int32, (NB, NB), 1) + 1
    ).astype(F32)
    index = lax.broadcasted_iota(jnp.int32, (8, 2 * NB), 0)
    work = jnp.concatenate([table[at : at + NB, at : at + NB], eye], axis=1)
    groups = [work[k : k + 8, :] for k in range(0, NB, 8)]
    wide = (8, 2 * NB)
    for j in range(0, NB, 2):
        own, spot = divmod(j, 8)
        ones = [jnp.broadcast_to(groups[k][:, j : j + 1], wide) for k in range(own, NB // 8)]
        twos = [jnp.broadcast_to(groups[k][:, j + 1 : j + 2], wide) for k in range(own, NB // 8)]
        row1, row2 = groups[own][spot : spot + 1, :], groups[own][spot + 1 : spot + 2, :]
        a, b = ones[0][spot : spot + 1, :], twos[0][spot : spot + 1, :]
        d = twos[0][spot + 1 : spot + 2, :]
        inverse = 1.0 / (a * d - b * b)
        first = (d * row1 - b * row2) * inverse
        second = (a * row2 - b * row1) * inverse
        for k in range(own, NB // 8):
            change = ones[k - own] * first + twos[k - own] * second
            if k == own:
                change = jnp.where(index > spot + 1, change, 0.0)
            groups[k] = groups[k] - change
    work = jnp.concatenate(groups, axis=0)
    odd = lax.rem(lax.broadcasted_iota(jnp.int32, (NB, 1), 0), 2) == 1
    pivot = jnp.sum(work[:, :NB] * eye, axis=1, keepdims=True)
    cross = jnp.sum(work[:, :NB] * back, axis=1, keepdims=True)
    right = work[:, NB:]
    before = jnp.concatenate([right[:1], right[:-1]], axis=0)
    ratio = jnp.where(odd, cross / jnp.concatenate([pivot[:1], pivot[:-1]], axis=0), 0.0)
    small = (right - ratio * before) * lax.rsqrt(pivot - ratio * cross)
    low, high = at // 128 * 128, size + -(-(at + NB) // 128) * 128
    rows = jnp.dot(small, table[at : at + NB, low:high], precision=HIGH, preferred_element_type=F32)
    table[at : at + NB, low:high] = rows
    if at + NB < size:
        below = rows[:, at + NB - low : size - low]
        table[at + NB :, low:high] = table[at + NB :, low:high] - inner(below, rows)


def set_table(table, gram):
    size = gram.shape[0]
    table[:, :size] = gram
    table[:, size:] = (
        lax.broadcasted_iota(jnp.int32, (size, size), 0)
        == lax.broadcasted_iota(jnp.int32, (size, size), 1)
    ).astype(F32)


def inverse_of(table, gram):
    set_table(table, gram)
    for at in range(0, gram.shape[0], NB):
        factor_block(table, at)
    return table[:, gram.shape[0] :]


MESH = pl.DeviceIdType.MESH
VMEM = pl.BlockSpec(memory_space=pltpu.VMEM)
ANY = pl.BlockSpec(memory_space=pl.ANY)


def place():
    tok, row = lax.axis_index("tok"), lax.axis_index("row")
    return tok, row, row // 2, lax.rem(row, 2)


def other(index, bit):
    if bit == 1:
        return index + 1 - 2 * lax.rem(index, 2)
    return lax.rem(index + 2, 4)


def greet(partners):
    barrier = pltpu.get_barrier_semaphore()
    for partner in partners:
        pl.semaphore_signal(barrier, inc=1, device_id=partner, device_id_type=MESH)
    pl.semaphore_wait(barrier, len(partners))


def remote(src, dst, send_sem, recv_sem, partner):
    return pltpu.make_async_remote_copy(
        src_ref=src, dst_ref=dst, send_sem=send_sem, recv_sem=recv_sem,
        device_id=partner, device_id_type=MESH,
    )


def split_two(block):
    first = block.astype(BF16)
    return first, (block - first.astype(F32)).astype(BF16)


def split_three(block):
    first, rest = block.astype(BF16), None
    rest = block - first.astype(F32)
    second = rest.astype(BF16)
    third = (rest - second.astype(F32)).astype(BF16)
    return first, second, third


def acts_kernel(
    hidden_hbm, resid_hbm, din_hbm, dout_hbm, acts_ref,
    hidden_ref, resid_ref, din_ref, dout_ref,
    part, inbox, code, load_sem, sum_send, sum_recv, code_send, code_recv,
):
    tok, row, _, _ = place()
    loads = [
        pltpu.make_async_copy(source, target, load_sem.at[i])
        for i, (source, target) in enumerate(
            (
                (din_hbm, din_ref),
                (hidden_hbm, hidden_ref),
                (dout_hbm, dout_ref),
                (resid_hbm, resid_ref),
            )
        )
    ]
    for load in loads:
        load.start()
    share = hidden_ref.shape[0] // 8
    peers = [(tok, lax.rem(row + d, 8)) for d in range(1, 8)]
    greet(peers)

    loads[0].wait()
    loads[1].wait()
    part[...] = jnp.dot(hidden_ref[...], din_ref[...], preferred_element_type=F32)
    copies = []
    for d, peer in enumerate(peers):
        piece = part.at[pl.ds(pl.multiple_of(peer[1] * share, 8), share)]
        copies.append(remote(piece, inbox.at[d], sum_send.at[d], sum_recv.at[d], peer))
        copies[-1].start()
    mine = pl.ds(pl.multiple_of(row * share, 8), share)
    total = part[mine, :]
    for d in range(7):
        copies[d].wait_recv()
        total += inbox[d]
    code[mine, :] = total
    gathers = []
    for d, peer in enumerate(peers):
        gathers.append(remote(code.at[mine], code.at[mine], code_send.at[d], code_recv.at[d], peer))
        gathers[-1].start()
    for d in range(7):
        source = pl.ds(pl.multiple_of(lax.rem(row + 7 - d, 8) * share, 8), share)
        remote(code.at[source], code.at[source], code_send.at[d], code_recv.at[d], peers[d]).wait_recv()
    loads[2].wait()
    loads[3].wait()
    first, second, third = split_three(code[...])
    weight = dout_ref[...]
    own = jnp.dot(third, weight, preferred_element_type=F32)
    own += jnp.dot(second, weight, preferred_element_type=F32)
    own += jnp.dot(first, weight, preferred_element_type=F32)
    acts_ref[...] = resid_ref[...].astype(F32) + own
    for copy in copies + gathers:
        copy.wait_send()


def activation_rows(hidden, resid, down_in, down_out):
    rows, width = resid.shape
    rank = down_in.shape[1]
    dma = pltpu.SemaphoreType.DMA
    return pl.pallas_call(
        acts_kernel,
        in_specs=[ANY] * 4,
        out_specs=VMEM,
        out_shape=jax.ShapeDtypeStruct((rows, width), F32),
        scratch_shapes=[
            pltpu.VMEM(hidden.shape, BF16),
            pltpu.VMEM(resid.shape, BF16),
            pltpu.VMEM(down_in.shape, BF16),
            pltpu.VMEM(down_out.shape, BF16),
            pltpu.VMEM((rows, rank), F32),
            pltpu.VMEM((7, rows // 8, rank), F32),
            pltpu.VMEM((rows, rank), F32),
            dma((4,)), dma((7,)), dma((7,)), dma((7,)), dma((7,)),
        ],
        compiler_params=pltpu.CompilerParams(
            collective_id=1, has_side_effects=True, vmem_limit_bytes=60 * 2**20
        ),
    )(hidden, resid, down_in, down_out)


CUTS = 8
LAG = 4


DIAGONAL = 16
FIRST = 23
HOP = 5
STEP = 4
SHARE = 56


def applied_kernel(
    own_ref, weight_ref, start_ref, out_ref, high_ref, low_ref, packed_ref,
    base, held, begin, image, own, inner_in, line_in, stage,
    gp, xp, own_x, inner_x, line_x, stage_x, x_in,
    move_send, move_recv, weight_sem, begin_sem, pair_send, pair_recv, line_send, line_recv, out_sem,
    xp_send, xp_recv, xl_send, xl_recv, xs_send, xs_recv, bc_send, bc_recv, tk_send, tk_recv, last_send, last_recv,
):
    tok, row, z, core = place()
    rows = own_ref.shape[0]
    _, steps, _, width = own.shape
    tokens = 4 * rows
    rank = begin.shape[2]
    cut = rows // CUTS
    quarter, strip = rows // 4, rows // 4 * rank // tokens
    sibling = (tok, other(row, 1))
    toks = [tok, other(tok, 1), other(tok, 2), other(other(tok, 1), 2)]
    by_x, by_y = (toks[1], row), (toks[2], row)
    down, up = (tok, row - 2), (tok, row + 2)
    barrier = pltpu.get_barrier_semaphore()
    for partner in [sibling] + [(t, row) for t in toks[1:]]:
        pl.semaphore_signal(barrier, inc=1, device_id=partner, device_id_type=MESH)

    @pl.when(z > 0)
    def _():
        pl.semaphore_signal(barrier, inc=1, device_id=down, device_id_type=MESH)

    @pl.when(z < 3)
    def _():
        pl.semaphore_signal(barrier, inc=1, device_id=up, device_id_type=MESH)

    pl.semaphore_wait(barrier, jnp.where((z == 0) | (z == 3), 5, 6))

    def block_of(step, which):
        side = core if which // 2 else 1 - core
        return 4 * (which % 2) + 2 * lax.rem(step, 2) + side

    def load(step, which):
        columns = pl.ds(pl.multiple_of(block_of(step, which) * width, 128), width)
        return pltpu.make_async_copy(weight_ref.at[:, columns], held.at[which % 2], weight_sem.at[which % 2])

    def load_begin(step, which):
        lines = pl.ds(pl.multiple_of(block_of(step, which) * width, 16), width)
        return pltpu.make_async_copy(start_ref.at[lines], begin.at[which % 2], begin_sem.at[which % 2])

    for which in range(2):
        load(0, which).start()

    half = rows // 2
    top, bottom = pl.ds(0, half), pl.ds(half, half)

    def move(index):
        source, to, piece, partner = (
            (own_ref, 0, top, by_x),
            (own_ref, 1, bottom, by_y),
            (own_ref, 0, bottom, by_x),
            (own_ref, 1, top, by_y),
            (base.at[0], 2, top, by_y),
            (base.at[1], 2, bottom, by_x),
        )[index]
        return remote(
            source.at[piece], base.at[to, piece], move_send.at[index], move_recv.at[index], partner
        )

    for index in range(4):
        move(index).start()

    def emit(value, group):
        at = pl.ds(pl.multiple_of(group * rows, 16), rows)
        first, second = split_two(value)
        high_ref[at, :] = first
        low_ref[at, :] = second

    emit(own_ref[...], tok)
    image[...] = jnp.zeros_like(image)

    def group_of(step):
        slot = step // 2
        across = lax.rem(lax.rem(tok, 2) + lax.rem(slot, 2), 2)
        return 2 * lax.rem(tok // 2 + slot // 2, 2) + across

    def pair_copy(step, end):
        return remote(
            stage.at[end], inner_in.at[end, step], pair_send.at[end], pair_recv.at[end, step], sibling
        )

    def line_copy(end, step, piece, at):
        part = pl.ds(pl.multiple_of(piece * cut, 8), cut)
        return remote(
            own.at[end, step, part], line_in.at[end, step, part], line_send.at[end],
            line_recv.at[end, at], down if end == 0 else up,
        )

    def out_copy(end, step):
        part = pl.ds(pl.multiple_of(group_of(step) * rows, 8), rows)
        return pltpu.make_async_copy(own.at[end, step], out_ref.at[lax.rem(step, 2), part], out_sem.at[step])

    def multiply(step, which):
        part = pl.ds(pl.multiple_of(group_of(step) * rows, 16), rows)
        end = which % 2
        load(step, which).wait()
        weight = held[which % 2]
        value = jnp.dot(low_ref[part, :], weight, preferred_element_type=F32)
        value += jnp.dot(high_ref[part, :], weight, preferred_element_type=F32)
        if which < 2:

            @pl.when(step >= 1)
            def _():
                pair_copy(step - 1, end).wait_send()

            stage[end] = value
            pair_copy(step, end).start()
        else:
            own[end, step] = value

        @pl.when((step >= 1) & (step < 3))
        def _():
            load_begin(step, which).wait()
            image[...] = image[...] + jnp.dot(
                held[which % 2], begin[which % 2], preferred_element_type=F32
            )

        following, next_which = (step, which + 2) if which < 2 else (step + 1, which - 2)

        @pl.when(following < steps)
        def _():
            load(following, next_which).start()

        @pl.when((following >= 1) & (following < 3))
        def _():
            load_begin(following, next_which).start()

    hops_of = [3 - z, z]

    def forward(end, at):
        hops = hops_of[end]
        at = at - LAG * hops

        @pl.when((at >= 0) & (at < CUTS * steps))
        def _():
            step, piece = at // CUTS, lax.rem(at, CUTS)
            part = pl.ds(pl.multiple_of(piece * cut, 8), cut)

            @pl.when(piece == 0)
            def _():
                pair_copy(step, end).wait_recv()

            own[end, step, part, :] = own[end, step, part, :] + inner_in[end, step, part, :]

            @pl.when(hops > 0)
            def _():
                line_copy(end, step, piece, at).wait_recv()
                own[end, step, part, :] = own[end, step, part, :] + line_in[end, step, part, :]

            @pl.when(hops < 3)
            def _():
                line_copy(end, step, piece, at).start()

            @pl.when((hops == 3) & (piece == CUTS - 1))
            def _():
                out_copy(end, step).start()

    def x_pair(end):
        return remote(stage_x.at[end], inner_x.at[end], xp_send.at[end], xp_recv.at[end], sibling)

    def x_line(end):
        return remote(
            own_x.at[end], line_x.at[end], xl_send.at[end], xl_recv.at[end], down if end == 0 else up
        )

    def x_sum(d):
        piece = pl.ds(pl.multiple_of(rows * toks[d], 8), rows)
        return remote(xp.at[piece], x_in.at[d - 1], xs_send.at[d - 1], xs_recv.at[d - 1], (toks[d], row))

    def spread(end):
        piece = packed_ref.at[end, core, tok]
        return remote(piece, piece, bc_send.at[end], bc_recv.at[end], up if end == 0 else down)

    def token_spread(end, d):
        piece = packed_ref.at[end, core, tok]
        return remote(piece, piece, tk_send.at[end, d], tk_recv.at[end, d], (toks[d], row))

    def token_landing(end, d):
        piece = packed_ref.at[end, core, toks[d]]
        return remote(piece, piece, tk_send.at[end, d], tk_recv.at[end, d], (toks[d], row))

    def last_copy(end, side):
        piece = packed_ref.at[end, side]
        return remote(piece, piece, last_send.at[end], last_recv.at[end], sibling)

    def x_fill():
        mine = pl.ds(pl.multiple_of(rows * tok, 8), rows)
        total = xp[mine, :]
        for d in (1, 2, 3):
            x_sum(d).wait_recv()
            total += x_in[d - 1]
        xp[mine, :] = total
        for end in range(2):
            for target, side in ((own_x, core), (stage_x, 1 - core)):
                place_of = 2 * end + side
                at = pl.ds(pl.multiple_of(place_of * quarter, 8), quarter)
                target[end, :quarter, :] = gp[at, :]
                for m in range(tokens // rank):
                    lines = pl.ds(pl.multiple_of(tok * rows + place_of * quarter + m * strip, 8), strip)
                    target[end, quarter:, m * rank : (m + 1) * rank] = xp[lines, :]
            x_pair(end).start()

    def small(step, piece):
        def on(when, extra, action):
            when = when * CUTS // 8
            if piece == when % CUTS:
                pl.when((step == when // CUTS) & extra)(action)

        def arrive_first():
            for index in (0, 1):
                move(index).wait_recv()
                move(4 + index).start()

        def arrive_x():
            move(2).wait_recv()
            emit(base[0], toks[1])

        def arrive_y():
            move(3).wait_recv()
            emit(base[1], toks[2])

        def arrive_diagonal():
            move(4).wait_recv()
            move(5).wait_recv()
            emit(base[2], toks[3])

        def gram():
            mine = pl.ds(pl.multiple_of(tok * rows, 16), rows)
            gp[...] = dots((high_ref[mine, :], low_ref[mine, :]), (high_ref[...], low_ref[...]), ((1,), (1,)))

        def imaged():
            xp[...] = dots((high_ref[...], low_ref[...]), split_two(image[...]), ((1,), (0,)))
            for d in (3, 1, 2):
                x_sum(d).start()

        always = step >= 0
        on(4, always, arrive_first)
        on(7, always, arrive_x)
        on(12, always, arrive_y)
        on(DIAGONAL, always, arrive_diagonal)
        on(DIAGONAL + 1, always, imaged)
        on(DIAGONAL + 2, always, gram)
        on(FIRST - 2, always, x_fill)
        for end in range(2):
            hops = hops_of[end]

            def joined(end=end):
                x_pair(end).wait_recv()
                own_x[end] = own_x[end] + inner_x[end]

            on(FIRST, always, joined)

            def passed(end=end):
                x_line(end).wait_recv()
                own_x[end] = own_x[end] + line_x[end]

            def passed_on(end=end):
                passed(end)
                x_line(end).start()

            on(FIRST, hops == 0, lambda end=end: x_line(end).start())
            on(FIRST + HOP, hops == 1, passed_on)
            on(FIRST + 2 * HOP, hops == 2, passed_on)

            def to_tokens(end=end):
                for d in (3, 1, 2):
                    token_spread(end, d).start()

            def packed(end=end):
                passed(end)
                packed_ref[end, core, tok] = own_x[end]
                spread(end).start()
                to_tokens(end)

            def relay(end=end):
                spread(end).wait_recv()
                spread(end).start()
                to_tokens(end)

            def relay_end(end=end):
                spread(end).wait_recv()
                to_tokens(end)

            on(FIRST + 3 * HOP, hops == 3, packed)
            on(FIRST + 3 * HOP + STEP, hops == 2, relay)
            on(FIRST + 3 * HOP + 2 * STEP, hops == 1, relay)
            on(FIRST + 3 * HOP + 3 * STEP, hops == 0, relay_end)

        def share_out():
            for end in range(2):
                for d in (1, 2, 3):
                    token_landing(end, d).wait_recv()
                last_copy(end, core).start()

        on(SHARE, always, share_out)

    for which in range(4):
        multiply(0, which)

    def one(step, carry):
        for piece in range(CUTS):
            for which in range(4):
                if piece == which * CUTS // 4:

                    @pl.when(step + 1 < steps)
                    def _():
                        multiply(step + 1, which)

            for end in range(2):
                forward(end, step * CUTS + piece)
            small(step, piece)
        return carry

    lax.fori_loop(0, steps + -(-3 * LAG // CUTS), one, 0)

    for index in range(6):
        move(index).wait_send()
    for d in (1, 2, 3):
        x_sum(d).wait_send()
    for end in range(2):
        hops = hops_of[end]
        last_copy(end, 1 - core).wait_recv()
        last_copy(end, core).wait_send()
        x_pair(end).wait_send()
        for d in (1, 2, 3):
            token_spread(end, d).wait_send()
        pair_copy(steps - 1, end).wait_send()

        @pl.when(hops < 3)
        def _():
            x_line(end).wait_send()
            remote(
                own.at[end], line_in.at[end], line_send.at[end], line_recv.at[end, 0],
                down if end == 0 else up,
            ).wait_send()

        @pl.when(hops > 0)
        def _():
            spread(end).wait_send()

        @pl.when(hops == 3)
        def _():
            for step in range(steps):
                out_copy(end, step).wait()


def applied_sums(acts, weight, start):
    rows, depth = acts.shape
    tokens = 4 * rows
    width = weight.shape[1] // 8
    rank = start.shape[1]
    steps = 8
    quarter = rows // 4
    strip = quarter * rank // tokens
    slab = quarter + strip
    dma = pltpu.SemaphoreType.DMA
    return pl.pallas_call(
        applied_kernel,
        in_specs=[VMEM, ANY, ANY],
        out_specs=[ANY, VMEM, VMEM, VMEM],
        out_shape=[
            jax.ShapeDtypeStruct((2, tokens, width), F32),
            jax.ShapeDtypeStruct((tokens, depth), BF16),
            jax.ShapeDtypeStruct((tokens, depth), BF16),
            jax.ShapeDtypeStruct((2, 2, 4, quarter + strip, tokens), F32),
        ],
        scratch_shapes=[
            pltpu.VMEM((3, rows, depth), F32),
            pltpu.VMEM((2, depth, width), BF16),
            pltpu.VMEM((2, width, rank), BF16),
            pltpu.VMEM((depth, rank), F32),
            pltpu.VMEM((2, steps, rows, width), F32),
            pltpu.VMEM((2, steps, rows, width), F32),
            pltpu.VMEM((2, steps, rows, width), F32),
            pltpu.VMEM((2, rows, width), F32),
            pltpu.VMEM((rows, tokens), F32),
            pltpu.VMEM((tokens, rank), F32),
            pltpu.VMEM((2, slab, tokens), F32),
            pltpu.VMEM((2, slab, tokens), F32),
            pltpu.VMEM((2, slab, tokens), F32),
            pltpu.VMEM((2, slab, tokens), F32),
            pltpu.VMEM((3, rows, rank), F32),
            dma((6,)), dma((6,)), dma((2,)), dma((2,)), dma((2,)), dma((2, steps)), dma((2,)),
            dma((2, steps * CUTS)), dma((steps,)),
            dma((2,)), dma((2,)), dma((2,)), dma((2,)), dma((3,)), dma((3,)), dma((2,)), dma((2,)),
            dma((2, 4)), dma((2, 4)), dma((2,)), dma((2,)),
        ],
        compiler_params=pltpu.CompilerParams(
            collective_id=2, has_side_effects=True, vmem_limit_bytes=60 * 2**20
        ),
        cost_estimate=pl.CostEstimate(
            flops=4 * tokens * depth * weight.shape[1],
            bytes_accessed=500 * 2**20,
            transcendentals=0,
        ),
    )(acts, weight, start)


TRI = ((0, 0), (1, 0), (1, 1), (2, 0), (2, 1), (2, 2))


def basis_kernel(
    blocks_ref, packed_ref, high_ref, low_ref, left_ref, right_ref, core_ref,
    grams, parts, square, pair_in, sum_in, whole, halves, tall, sent, landed, table,
    pair_send, pair_recv, sum_send, sum_recv, line_send, line_recv, tok_send, tok_recv, end_send, end_recv,
    *, features, columns,
):
    tok, row, z, core = place()
    _, tokens, rank = tall.shape
    width = blocks_ref.shape[2]
    third = tokens // 3
    piece = 6 * third // 16
    half = 8 * piece
    end = z // 2
    holds = (z == 0) | (z == 3)
    sibling = (tok, other(row, 1))
    toks = [tok, other(tok, 1), other(tok, 2), other(other(tok, 1), 2)]
    barrier = pltpu.get_barrier_semaphore()
    near = [sibling] + [(t, row) for t in toks[1:]] + [(tok, lax.rem(row + d, 8)) for d in (2, 4, 6)]
    for partner in near:
        pl.semaphore_signal(barrier, inc=1, device_id=partner, device_id_type=MESH)
    far = [(t, 6 - 2 * z + core) for t in toks[1:]]

    @pl.when(holds)
    def _():
        for partner in far:
            pl.semaphore_signal(barrier, inc=1, device_id=partner, device_id_type=MESH)

    pl.semaphore_wait(barrier, jnp.where(holds, 10, 7))

    mine = pl.ds(pl.multiple_of(core * half, 8), half)
    theirs = pl.ds(pl.multiple_of((1 - core) * half, 8), half)
    pair = remote(square.at[theirs], pair_in, pair_send.at[0], pair_recv.at[0], sibling)

    @pl.when(holds)
    def _():
        for at in range(2):
            first, second = split_two(blocks_ref[at])
            parts[0, at] = first
            parts[1, at] = second
        for n, (i, j) in enumerate(TRI):
            a, b = pl.ds(i * third, third), pl.ds(j * third, third)
            square[pl.ds(n * third, third), :] = sum(
                dots((parts[0, at, a], parts[1, at, a]), (parts[0, at, b], parts[1, at, b]), ((1,), (1,)))
                for at in range(2)
            )
        pair.start()

    quarter, strip = tokens // 16, tokens // 16 * rank // tokens
    for a in range(2):
        for b in range(2):
            for c in range(4):
                first, second = split_two(packed_ref[a, b, c, :quarter, :])
                at = pl.ds((4 * c + 2 * a + b) * quarter, quarter)
                grams[0, at, :] = first
                grams[1, at, :] = second
                for m in range(tokens // rank):
                    lines = pl.ds((4 * c + 2 * a + b) * quarter + m * strip, strip)
                    tall[1, lines, :] = (
                        packed_ref[a, b, c, quarter:, m * rank : (m + 1) * rank] / tokens
                    )
    gram_parts = (grams[0], grams[1])
    block = tall[1]
    tall[0] = dots(gram_parts, split_two(block), ((1,), (0,)))
    set_table(table, inner(block, tall[0]))

    def spot(to_core, to_tok, to_end):
        return pl.ds(pl.multiple_of(to_core * half + (to_tok * 2 + to_end) * piece, 8), piece)

    def sum_copy(d):
        to_tok = toks[d // 2]
        to_end = 1 - end if d % 2 else end
        return remote(
            square.at[spot(core, to_tok, to_end)], sum_in.at[d], sum_send.at[d], sum_recv.at[d],
            (to_tok, 6 * to_end + core),
        )

    @pl.when(holds)
    def _():
        pair.wait_recv()
        square[mine, :] = square[mine, :] + pair_in[...]
        for d in (7, 5, 3, 1, 6, 4, 2):
            sum_copy(d).start()

    factor_block(table, 0)
    factor_block(table, NB)

    here = spot(core, tok, end)

    def line_copy(i):
        to = (3 - i) + end * (2 * i - 3)
        return remote(whole.at[here], whole.at[here], line_send.at[i], line_recv.at[end], (tok, 2 * to + core))

    def tok_copy(source_end, d):
        place_of = spot(core, tok, source_end)
        return remote(
            whole.at[place_of], whole.at[place_of], tok_send.at[source_end, d], tok_recv.at[source_end, d],
            (toks[d], row),
        )

    @pl.when(holds)
    def _():
        total = square[here, :]
        for d in range(1, 8):
            sum_copy(d).wait_recv()
            total += sum_in[d]
        whole[here, :] = total
        for i in range(3):
            line_copy(i).start()
        for d in (3, 1, 2):
            tok_copy(end, d).start()

    factor_block(table, 2 * NB)
    for source in range(2):

        @pl.when(z != 3 * source)
        def _():
            landing = spot(core, tok, source)
            remote(
                whole.at[landing], whole.at[landing], line_send.at[0], line_recv.at[source], sibling
            ).wait_recv()
            for d in (3, 1, 2):
                tok_copy(source, d).start()

    factor_block(table, 3 * NB)
    tall[1] = turned(tall[0], table[:, rank:]) / tokens
    for source in range(2):
        for d in (1, 2, 3):
            landing = spot(core, toks[d], source)
            remote(
                whole.at[landing], whole.at[landing], tok_send.at[source, d], tok_recv.at[source, d], sibling
            ).wait_recv()
    last = remote(whole.at[mine], whole.at[mine], pair_send.at[1], pair_recv.at[1], sibling)
    last.start()
    remote(whole.at[theirs], whole.at[theirs], pair_send.at[1], pair_recv.at[1], sibling).wait_recv()
    first, second = split_two(whole[...])
    halves[0] = first
    halves[1] = second

    def squared(to, block):
        pieces = [split_two(block[i * third : (i + 1) * third, :]) for i in range(3)]
        for i in range(3):
            total = None
            for j in range(3):
                n = TRI.index((max(i, j), min(i, j)))
                at = pl.ds(n * third, third)
                dims = ((1,), (0,)) if i >= j else ((0,), (0,))
                term = dots((halves[0, at], halves[1, at]), pieces[j], dims)
                total = term if total is None else total + term
            tall[to, pl.ds(i * third, third), :] = total

    block = tall[1]
    squared(0, block)
    inverse = inverse_of(table, inner(block, tall[0]))
    tall[1] = turned(tall[0], inverse) / tokens

    block = tall[1]
    tall[0] = dots(gram_parts, split_two(block), ((1,), (0,)))
    inverse = inverse_of(table, inner(block, tall[0]))
    coef = split_two(turned(block, inverse))
    tall[1] = turned(tall[0], inverse) / tokens

    block = tall[1]
    ends = split_two(block)
    carry = remote(
        sent, landed, end_send.at[0], end_recv.at[0],
        (tok, jnp.where(z < 2, 2, 4) + core),
    )

    @pl.when(holds)
    def _():
        away = 1 - end
        sent[...] = dots((parts[0, away], parts[1, away]), ends, ((0,), (0,)))
        carry.start()
        landed[...] = dots((parts[0, end], parts[1, end]), ends, ((0,), (0,)))

    left_ref[...] = math.sqrt(features) * dots((high_ref[...], low_ref[...]), coef, ((0,), (0,)))
    squared(0, block)
    gram = inner(block, tall[0])
    inverse = inverse_of(table, gram)
    core_ref[...] = outer(gram, inverse)

    @pl.when(z == 1)
    def _():
        carry.wait_recv()

    @pl.when(z == 2)
    def _():
        carry.wait_recv()

    right_ref[...] = math.sqrt(columns) * turned(landed[...], inverse)

    @pl.when(holds)
    def _():
        carry.wait_send()
        pair.wait_send()
        for d in range(1, 8):
            sum_copy(d).wait_send()
        for i in range(3):
            line_copy(i).wait_send()

    for source in range(2):
        for d in (1, 2, 3):
            tok_copy(source, d).wait_send()
    last.wait_send()


def bases(blocks, packed, high, low, rank, features, columns):
    tokens = high.shape[0]
    width, depth = blocks.shape[2], high.shape[1]
    third = tokens // 3
    dma = pltpu.SemaphoreType.DMA
    return pl.pallas_call(
        functools.partial(basis_kernel, features=features, columns=columns),
        in_specs=[VMEM] * 4,
        out_specs=[VMEM] * 3,
        out_shape=[
            jax.ShapeDtypeStruct((depth, rank), F32),
            jax.ShapeDtypeStruct((width, rank), F32),
            jax.ShapeDtypeStruct((rank, rank), F32),
        ],
        scratch_shapes=[
            pltpu.VMEM((2, tokens, tokens), BF16),
            pltpu.VMEM((2, 2, tokens, width), BF16),
            pltpu.VMEM((6 * third, third), F32),
            pltpu.VMEM((3 * third, third), F32),
            pltpu.VMEM((8, 6 * third // 16, third), F32),
            pltpu.VMEM((6 * third, third), F32),
            pltpu.VMEM((2, 6 * third, third), BF16),
            pltpu.VMEM((2, tokens, rank), F32),
            pltpu.VMEM((width, rank), F32),
            pltpu.VMEM((width, rank), F32),
            pltpu.VMEM((rank, 2 * rank), F32),
            dma((2,)), dma((2,)), dma((8,)), dma((8,)), dma((3,)), dma((2,)),
            dma((2, 4)), dma((2, 4)), dma((1,)), dma((1,)),
        ],
        compiler_params=pltpu.CompilerParams(
            collective_id=3, has_side_effects=True, vmem_limit_bytes=56 * 2**20
        ),
    )(blocks, packed, high, low)


def token_space(hidden, resid, down_in, down_out, up_weight, start):
    features = up_weight.shape[0] * 8
    columns = up_weight.shape[1] * 4
    acts = activation_rows(hidden, resid, down_in, down_out)
    blocks, high, low, packed = applied_sums(acts, up_weight, start)
    return bases(blocks, packed, high, low, start.shape[1], features, columns)


def shards(hidden, *rest):
    tokens = hidden.shape[0] * lax.axis_size("tok")
    if tokens > 1024 or (lax.axis_size("tok"), lax.axis_size("row")) != (4, 8):
        return feature_space(hidden, *rest)
    return token_space(hidden, *rest)


def solution(mesh):
    placed = (
        P("tok", "row"),
        P("tok", "row"),
        P("row", None),
        P(None, "row"),
        P("row", "tok"),
        P("tok", None),
    )
    return jax.shard_map(
        shards,
        mesh=mesh,
        in_specs=placed,
        out_specs=(P("row", None), P(("tok", "row"), None), P()),
        check_vma=False,
    )
```
